512 devices in a mesh: group: 16 (over y, z_hi), member: 32 (over z_lo, x, core).
Axes of the slice: x: 4, y: 8, z: 8 (z_hi: 2, z_lo: 4; z = z_hi * 4 + z_lo), core: 2. Of those that a mesh axis runs over, the one named last changes fastest.
Arguments:
- queries: float32 [4096, 768], P(('group', 'member')), may hold values from -6 to 6
- centroids: float32 [16384, 768], P(('group', 'member')), may hold values from -0.21875 to 0.21875
- stored: float32 [64, 2048, 768], P('group', 'member'), may hold values from -0.21875 to 0.21875
- vector_ids: int32 [64, 2048], P('group', 'member'), may hold values from -1 to 131071, as said below
- list_home: int32 [64], replicated, may hold values from 0 to 63, as said below
- probes: int32 [16, 3, 16], replicated, may hold values from 0 to 63, as said below
Outputs:
- coarse_best: float32 [4096], P(('group', 'member'))
- fine_best: float32 [3, 4096], P(None, ('group', 'member'))
The draws below stay inside these ranges and needn't reach their ends.
Inputs may be any that keep to these rules, and one draw needn't show every extreme that they name: A permutation: list l is stored at slot list_home[l], and slot t belongs to group t // 4. `probes`: for each block and step the 16 probed lists are stored in 16 different groups, one in each. `vector_ids`: ids are distinct where not -1; each list has its valid vectors first, 256 or more of them.
All inputs are finite; a program needn't handle non-finite values.
Results may differ from the reference program's by a relative error of at most 0.0003.
Values sent between devices are 32-bit elements; how exact they have to be, the bound alone decides.
A program may use at most 64 MiB of HBM per device.

```python
import jax
import jax.numpy as jnp
from jax import lax

D = 768
LG = 4
LEN = 2048
STEPS = 3
GROUPS = 16
BLOCK = 256
QUERIES = 4096
CENTROIDS = 16384
LISTS = 64


def probe_tables(key):
    home_slot = jax.random.permutation(jax.random.fold_in(key, 11), LISTS).astype(jnp.int32)
    at_slot = jnp.argsort(home_slot, stable=True).astype(jnp.int32)
    draw_one = jax.random.randint(jax.random.fold_in(key, 12), (GROUPS, STEPS, GROUPS), 0, LG)
    draw_two = jax.random.randint(jax.random.fold_in(key, 13), (GROUPS, STEPS, GROUPS), 0, LG)
    local_pick = jnp.minimum(draw_one, draw_two).astype(jnp.int32)
    owner_rank = jnp.arange(GROUPS, dtype=jnp.int32)[None, None, :]
    chosen = at_slot[owner_rank * LG + local_pick]
    row_keys = jax.random.split(jax.random.fold_in(key, 14), GROUPS * STEPS)
    orders = jax.vmap(lambda kk: jax.random.permutation(kk, GROUPS))(row_keys).reshape(GROUPS, STEPS, GROUPS)
    probe_ids = jnp.take_along_axis(chosen, orders.astype(jnp.int32), axis=2)
    return (home_slot, probe_ids.astype(jnp.int32))


def draw_list_home(key, part):
    home_slot, probe_ids = probe_tables(key)
    return home_slot


def draw_probes(key, part):
    home_slot, probe_ids = probe_tables(key)
    return probe_ids


def draw_vector_ids(key, part):
    shuffled = jax.random.permutation(jax.random.fold_in(key, 21), LISTS * LEN).astype(jnp.int32).reshape(LISTS, LEN)
    lengths = jax.random.randint(jax.random.fold_in(key, 22), (LISTS, 1), LEN // 8, LEN + 1)
    places = jnp.arange(LEN, dtype=jnp.int32)[None, :]
    return jnp.where(places < lengths, shuffled, -1).astype(jnp.int32)


def steps_of(rng, dims, shards, smallest, high):
    def one(position, blocks):
        heights = jax.random.uniform(jax.random.fold_in(jax.random.fold_in(rng, 6), position), (blocks,), jnp.float32, smallest / len(shards), high / len(shards))
        return jnp.repeat(jnp.exp(heights), dims[position] // blocks).reshape((-1,) + (1,) * (len(dims) - position - 1))

    loudness = one(*shards[0])
    for cut in shards[1:]:
        loudness = loudness * one(*cut)
    return loudness


def centred(stream_key, shape, deviation, limit, shards=(), kind=jnp.bfloat16):
    values = deviation * jax.random.normal(stream_key, shape, jnp.float32)
    if shards:
        values = values * steps_of(stream_key, shape, shards, -0.22, 0.18)
    return jnp.clip(values, -limit, limit).astype(kind)


def setup_inputs(seed: int = 0) -> dict:
    streams_of = jax.random.split(jax.random.key(seed), 7)
    queries = centred(streams_of[0], (QUERIES, D), 1.0, 6.0, ((0, 512),), jnp.float32)
    centroids = centred(streams_of[1], (CENTROIDS, D), D ** -0.5, 0.21875, ((0, 512),), jnp.float32)
    stored = centred(streams_of[2], (LISTS, LEN, D), D ** -0.5, 0.21875, ((0, 16), (1, 32)), jnp.float32)
    vector_ids = draw_vector_ids(jax.random.fold_in(streams_of[6], 71), 0)
    list_home = draw_list_home(jax.random.fold_in(streams_of[6], 71), 0)
    probes = draw_probes(jax.random.fold_in(streams_of[6], 71), 0)
    return dict(queries=queries, centroids=centroids, stored=stored, vector_ids=vector_ids, list_home=list_home, probes=probes)


def reference(queries, centroids, stored, vector_ids, list_home, probes):
    blocks = queries.reshape(GROUPS, BLOCK, D)

    def coarse_block(query_block):
        scores = jnp.einsum("qd,cd->qc", query_block, centroids, preferred_element_type=jnp.float32, precision=lax.Precision.HIGHEST)
        return jnp.max(scores, axis=1)

    coarse_best = lax.map(coarse_block, blocks).reshape(-1)

    def fine_group(pair_args):
        query_block, probe_rows = pair_args

        def one_step(list_row):
            slot_ids = list_home[list_row].astype(jnp.int32)
            vectors = stored[slot_ids].reshape(-1, D)
            usable = (vector_ids[slot_ids] >= 0).reshape(-1)
            scores = jnp.einsum("qd,rd->qr", query_block, vectors, preferred_element_type=jnp.float32, precision=lax.Precision.HIGHEST)
            scores = jnp.where(usable[None, :], scores, jnp.float32(-1e30))
            return jnp.max(scores, axis=1)

        return lax.map(one_step, probe_rows)

    fine_all = lax.map(fine_group, (blocks, probes))
    fine_best = jnp.transpose(fine_all, (1, 0, 2)).reshape(STEPS, -1)
    return coarse_best, fine_best
```

```python
import jax
import jax.numpy as jnp
from jax import lax
from jax.sharding import PartitionSpec as P

D = 768
STEPS = 3
AXES = ("group", "member")


def local(queries, centroids, stored, vector_ids, list_home, probes):
    member_pos = lax.axis_index("member")
    group_pos = lax.axis_index("group")
    members = lax.axis_size("member")
    rows_dev = queries.shape[0]
    lowest = jnp.float32(-1e30)
    every_query = lax.all_gather(queries, AXES, axis=0, tiled=True)
    lists_here, places = vector_ids.shape
    vectors = stored.reshape(-1, D)

    def score(rows):
        return jnp.einsum(
            "qd,rd->qr", every_query, rows, preferred_element_type=jnp.float32, precision=lax.Precision.HIGH
        )

    coarse = jnp.max(score(centroids), axis=1)
    usable = vector_ids.reshape(-1) >= 0
    fine = jnp.where(usable[None, :], score(vectors), lowest)
    per_list = jnp.max(fine.reshape(-1, lists_here, places), axis=2)

    slot_ids = list_home[probes]
    at_home = slot_ids // lists_here == group_pos
    local_slot = jnp.sum(jnp.where(at_home, slot_ids - group_pos * lists_here, 0), axis=2)
    blocks = local_slot.shape[0]
    chosen = local_slot[:, :, None] == jnp.arange(lists_here)[None, None, :]
    by_block = per_list.reshape(blocks, -1, lists_here)
    steps = [
        jnp.max(jnp.where(chosen[:, s][:, None, :], by_block, lowest), axis=2).reshape(-1) for s in range(STEPS)
    ]
    best = lax.pmax(jnp.stack([coarse] + steps), AXES)
    mine = lax.dynamic_slice_in_dim(best, (group_pos * members + member_pos) * rows_dev, rows_dev, 1)
    return mine[0], mine[1:]


def solution(mesh):
    placed = (
        P(AXES, None),
        P(AXES, None),
        P("group", "member", None),
        P("group", "member"),
        P(),
        P(),
    )
    return jax.shard_map(
        local,
        mesh=mesh,
        in_specs=placed,
        out_specs=(P(AXES), P(None, AXES)),
        check_vma=False,
    )
```

```python
import jax
import jax.numpy as jnp
from jax import lax
from jax.experimental import pallas as pl
from jax.experimental.pallas import tpu as pltpu
from jax.sharding import PartitionSpec as P

D = 768
STEPS = 3
AXES = ("group", "member")
LOW = -1e30
NX, NY, NZ, ZL = 4, 8, 8, 4
PART = D // 3
SIZES = (NX, NY, NZ)
X, Y, Z = 0, 1, 2
ORDERS = ((X, Y, Z), (Y, Z, X), (Z, X, Y))
VMEM_SPEC = pl.BlockSpec(memory_space=pltpu.VMEM)


def place():
    g, m = lax.axis_index("group"), lax.axis_index("member")
    x, y, core = (m // 2) % NX, g // 2, m % 2
    z = (g % 2) * ZL + m // (2 * NX)
    return [x, y, z], core


def device(at, core):
    x, y, z = at
    return (y * 2 + z // ZL, (z % ZL) * (2 * NX) + x * 2 + core)


def moved(at, axis, steps):
    size = SIZES[axis]
    out = list(at)
    out[axis] = lax.rem(at[axis] + (steps + size), size)
    return out


def greet(at, core):
    barrier = pltpu.get_barrier_semaphore()
    peers = [device(moved(at, axis, d), core) for axis in (X, Y, Z) for d in range(1, SIZES[axis])]
    return barrier, peers


def meet(barrier, peers):
    for peer in peers:
        pl.semaphore_signal(barrier, inc=1, device_id=peer, device_id_type=pl.DeviceIdType.MESH)
    pl.semaphore_wait(barrier, len(peers))


def gather_kernel(q, cent, stored, bias, out, cent_in, stored_in, bias_in, sends, recvs, local_sems):
    at, core = place()
    barrier, peers = greet(at, core)
    partner = device(at, 1 - core)
    meet(barrier, peers + [partner])
    used = [0]
    started = []

    def send(src, dst, to, sem):
        copy = pltpu.make_async_remote_copy(
            src_ref=src,
            dst_ref=dst,
            send_sem=sends.at[sem],
            recv_sem=recvs.at[sem],
            device_id=to,
            device_id_type=pl.DeviceIdType.MESH,
        )
        copy.start()
        started.append(copy)

    def arrived(slot, sem):
        pltpu.make_async_remote_copy(
            src_ref=slot,
            dst_ref=slot,
            send_sem=sends.at[sem],
            recv_sem=recvs.at[sem],
            device_id=partner,
            device_id_type=pl.DeviceIdType.MESH,
        ).wait_recv()

    def new_sem():
        used[0] += 1
        return used[0] - 1

    def columns(part):
        return q.at[:, pl.ds(part * PART, PART)]

    firsts = []
    for part, order in enumerate(ORDERS):
        mine = []
        for d in range(1, SIZES[order[0]]):
            sem = new_sem()
            slot = out.at[part, at[Z], at[Y], at[X]]
            send(columns(part), slot, device(moved(at, order[0], d), core), sem)
            fx, fy, fz = moved(at, order[0], -d)
            mine.append((out.at[part, fz, fy, fx], sem))
        firsts.append(mine)
    own = []
    for part in range(3):
        copy = pltpu.make_async_copy(columns(part), out.at[part, at[Z], at[Y], at[X]], local_sems.at[part])
        copy.start()
        own.append(copy)
    swaps = []
    for src, dst in ((stored, stored_in), (cent, cent_in), (bias, bias_in)):
        sem = new_sem()
        send(src, dst, partner, sem)
        swaps.append((dst, sem))

    def slab(part, phase, pos, half):
        x, y, z = at
        first = pl.ds(0 if half == 0 else (2 if (part, phase) == (0, 1) else 4), 2 if (part, phase) == (0, 1) else 4)
        if part == 0:
            return out.at[0, z, pos, first] if phase == 1 else out.at[0, pos, first]
        if part == 1:
            return out.at[1, pos, first, x] if phase == 1 else out.at[1, first, :, pos]
        return out.at[2, first, y, pos] if phase == 1 else out.at[2, first, pos]

    def ring(part, phase):
        axis = ORDERS[part][phase]
        size = SIZES[axis]
        last = size // 2
        streams = []
        for way in (1, -1):
            for turn in (0, 1):
                half = turn if way == 1 else 1 - turn
                hops = last if turn == 0 else last - 1
                streams.append((way, turn, half, hops, [new_sem() for _ in range(hops)]))

        def pos(offset):
            return lax.rem(at[axis] + (offset + size), size)

        def hop(stream, step):
            way, turn, half, hops, sems = stream
            piece = slab(part, phase, pos(-way * step), half)
            send(piece, piece, device(moved(at, axis, way), core), sems[step])

        def take(stream, step):
            way, turn, half, hops, sems = stream
            arrived(slab(part, phase, pos(-way * (step + 1)), half), sems[step])

        for turn in (0, 1):
            for stream in streams:
                if stream[1] == turn:
                    hop(stream, 0)
        if size == NX:
            yield
        for step in range(last):
            for turn in (0, 1):
                yield
                for stream in streams:
                    if stream[1] == turn and step < stream[3]:
                        take(stream, step)
                        if step + 1 < stream[3]:
                            hop(stream, step + 1)

    def whole(part):
        own[part].wait()
        for slot, sem in firsts[part]:
            arrived(slot, sem)
        yield from ring(part, 1)
        yield from ring(part, 2)

    running = [whole(0), whole(2), whole(1)]
    while running:
        for item in list(running):
            try:
                next(item)
            except StopIteration:
                running.remove(item)
    for slot, sem in swaps:
        arrived(slot, sem)
    for copy in started:
        copy.wait_send()


def score_kernel(g, st, st_in, ce, ce_in, bias, bias_in, chosen, out, high, low, base):
    lists = 4
    rows = st.shape[0]
    places = rows // lists
    cents = ce.shape[0]

    @pl.when(pl.program_id(0) == 0)
    def _():
        start = 0
        for ref in (st, st_in, ce, ce_in):
            count = ref.shape[0]
            top = ref[...].astype(jnp.bfloat16)
            high[start : start + count, :] = top
            low[start : start + count, :] = (ref[...] - top.astype(jnp.float32)).astype(jnp.bfloat16)
            start += count
        base[:rows, :128] = bias[...]
        base[:rows, 128:] = bias[...]
        base[rows : 2 * rows, :128] = bias_in[...]
        base[rows : 2 * rows, 128:] = bias_in[...]
        base[2 * rows :, :] = jnp.zeros((2 * cents, 256), jnp.float32)

    def dot(a, b):
        return lax.dot_general(a, b, (((1,), (1,)), ((), ())), preferred_element_type=jnp.float32)

    total = base[...]
    for part in range(3):
        q = g[part, 0].reshape(NY * NX * 8, PART)
        q_high = q.astype(jnp.bfloat16)
        q_low = (q - q_high.astype(jnp.float32)).astype(jnp.bfloat16)
        v_high = high[:, part * PART : (part + 1) * PART]
        v_low = low[:, part * PART : (part + 1) * PART]
        total = total + (dot(v_high, q_high) + (dot(v_high, q_low) + dot(v_low, q_high)))
    best = []
    for i in range(lists):
        a = jnp.max(total[i * places : (i + 1) * places], axis=0, keepdims=True)
        b = jnp.max(total[rows + i * places : rows + (i + 1) * places], axis=0, keepdims=True)
        best.append(jnp.maximum(a, b))
    out[0, 0:1, :] = jnp.max(total[2 * rows :], axis=0, keepdims=True)
    for s in range(STEPS):
        top = best[0] + chosen[0, s * lists : s * lists + 1, :]
        for i in range(1, lists):
            top = jnp.maximum(top, best[i] + chosen[0, s * lists + i : s * lists + i + 1, :])
        out[0, s + 1 : s + 2, :] = top


def reduce_kernel(part, out, from_z, from_x, from_y, mid_z, mid_x, sends, recvs):
    at, core = place()
    barrier, peers = greet(at, core)
    meet(barrier, peers)
    used = 0

    def swap(axis, source, landing, first):
        copies = []
        for d in range(1, SIZES[axis]):
            copy = pltpu.make_async_remote_copy(
                src_ref=source(d),
                dst_ref=landing.at[d - 1],
                send_sem=sends.at[first + d - 1],
                recv_sem=recvs.at[first + d - 1],
                device_id=device(moved(at, axis, d), core),
                device_id_type=pl.DeviceIdType.MESH,
            )
            copy.start()
            copies.append(copy)
        for copy in copies:
            copy.wait()

    def most(value, landing):
        for i in range(landing.shape[0]):
            value = jnp.maximum(value, landing[i])
        return value

    swap(Z, lambda d: part.at[lax.rem(at[Z] + d, NZ)], from_z, 0)
    mid_z[...] = most(part[at[Z]], from_z)
    swap(X, lambda d: mid_z, from_x, NZ - 1)
    mid_x[...] = most(mid_z[...], from_x)
    swap(Y, lambda d: mid_x, from_y, NZ + NX - 2)
    out[...] = most(mid_x[...], from_y)


def local(queries, centroids, stored, vector_ids, list_home, probes):
    (x, y, z), core = place()
    group_pos = lax.axis_index("group")
    lists, places = vector_ids.shape
    rows = lists * places
    cents = centroids.shape[0]
    f32 = jnp.float32
    vectors = stored.reshape(rows, D)
    bias = jnp.where(vector_ids.reshape(rows, 1) >= 0, f32(0), f32(LOW))
    bias = jnp.broadcast_to(bias, (rows, 128))

    slot_ids = list_home[probes]
    at_home = slot_ids // lists == group_pos
    local_slot = jnp.sum(jnp.where(at_home, slot_ids - group_pos * lists, 0), axis=2)
    chosen = local_slot[:, :, None] == jnp.arange(lists)[None, None, :]
    chosen = jnp.where(chosen, f32(0), f32(LOW)).reshape(NY, 2, STEPS * lists)
    chosen = jnp.transpose(chosen, (1, 2, 0))[:, None, :, :, None]
    chosen = jnp.broadcast_to(chosen, (2, ZL, STEPS * lists, NY, NX * 8)).reshape(NZ, STEPS * lists, NY * NX * 8)

    everything = (3, NZ, NY, NX, 8, PART)
    copies = 17 + 3 + 2 * 34
    gathered, cent_in, stored_in, bias_in = pl.pallas_call(
        gather_kernel,
        out_shape=[
            jax.ShapeDtypeStruct(everything, f32),
            jax.ShapeDtypeStruct((cents, D), f32),
            jax.ShapeDtypeStruct((rows, D), f32),
            jax.ShapeDtypeStruct((rows, 128), f32),
        ],
        in_specs=[VMEM_SPEC] * 4,
        out_specs=[VMEM_SPEC] * 4,
        scratch_shapes=[
            pltpu.SemaphoreType.DMA((copies,)),
            pltpu.SemaphoreType.DMA((copies,)),
            pltpu.SemaphoreType.DMA((3,)),
        ],
        compiler_params=pltpu.CompilerParams(collective_id=0, has_side_effects=True, vmem_limit_bytes=40 << 20),
        name="gather",
    )(queries, centroids, vectors, bias)

    def fixed(*shape):
        return pl.BlockSpec(shape, lambda i: (0,) * len(shape))

    partial = pl.pallas_call(
        score_kernel,
        grid=(NZ,),
        out_shape=jax.ShapeDtypeStruct((NZ, 1 + STEPS, NY * NX * 8), f32),
        in_specs=[
            pl.BlockSpec((3, 1, NY, NX, 8, PART), lambda i: (0, i, 0, 0, 0, 0)),
            fixed(rows, D),
            fixed(rows, D),
            fixed(cents, D),
            fixed(cents, D),
            fixed(rows, 128),
            fixed(rows, 128),
            pl.BlockSpec((1, STEPS * lists, NY * NX * 8), lambda i: (i, 0, 0)),
        ],
        out_specs=pl.BlockSpec((1, 1 + STEPS, NY * NX * 8), lambda i: (i, 0, 0)),
        scratch_shapes=[
            pltpu.VMEM((2 * rows + 2 * cents, D), jnp.bfloat16),
            pltpu.VMEM((2 * rows + 2 * cents, D), jnp.bfloat16),
            pltpu.VMEM((2 * rows + 2 * cents, 256), f32),
        ],
        compiler_params=pltpu.CompilerParams(vmem_limit_bytes=40 << 20),
        name="score",
    )(gathered, vectors, stored_in, centroids, cent_in, bias, bias_in, chosen)

    piece = (1 + STEPS, NY * NX * 8)
    best = pl.pallas_call(
        reduce_kernel,
        out_shape=jax.ShapeDtypeStruct(piece, f32),
        in_specs=[VMEM_SPEC],
        out_specs=VMEM_SPEC,
        scratch_shapes=[
            pltpu.VMEM((NZ - 1,) + piece, f32),
            pltpu.VMEM((NX - 1,) + piece, f32),
            pltpu.VMEM((NY - 1,) + piece, f32),
            pltpu.VMEM(piece, f32),
            pltpu.VMEM(piece, f32),
            pltpu.SemaphoreType.DMA((NX + NY + NZ - 3,)),
            pltpu.SemaphoreType.DMA((NX + NY + NZ - 3,)),
        ],
        compiler_params=pltpu.CompilerParams(collective_id=1, has_side_effects=True),
        name="reduce",
    )(partial)
    mine = lax.dynamic_slice_in_dim(best, (y * NX + x) * 8, 8, 1)
    return mine[0], mine[1:]


def solution(mesh):
    placed = (
        P(AXES, None),
        P(AXES, None),
        P("group", "member", None),
        P("group", "member"),
        P(),
        P(),
    )
    return jax.shard_map(
        local,
        mesh=mesh,
        in_specs=placed,
        out_specs=(P(AXES), P(None, AXES)),
        check_vma=False,
    )
```

```python
import jax
import jax.numpy as jnp
from jax import lax
from jax.experimental import pallas as pl
from jax.experimental.pallas import tpu as pltpu
from jax.sharding import PartitionSpec as P

D = 768
STEPS = 3
AXES = ("group", "member")
LOW = -1e30
NX, NY, NZ, ZL = 4, 8, 8, 4
PART = D // 3
SIZES = (NX, NY, NZ)
X, Y, Z = 0, 1, 2
ORDERS = ((X, Y, Z), (Y, Z, X), (Z, X, Y))
VMEM_SPEC = pl.BlockSpec(memory_space=pltpu.VMEM)


def place():
    g, m = lax.axis_index("group"), lax.axis_index("member")
    x, y, core = (m // 2) % NX, g // 2, m % 2
    z = (g % 2) * ZL + m // (2 * NX)
    return [x, y, z], core


def device(at, core):
    x, y, z = at
    return (y * 2 + z // ZL, (z % ZL) * (2 * NX) + x * 2 + core)


def moved(at, axis, steps):
    size = SIZES[axis]
    out = list(at)
    out[axis] = lax.rem(at[axis] + (steps + size), size)
    return out


def greet(at, core):
    barrier = pltpu.get_barrier_semaphore()
    peers = [device(moved(at, axis, d), core) for axis in (X, Y, Z) for d in range(1, SIZES[axis])]
    return barrier, peers


def meet(barrier, peers):
    for peer in peers:
        pl.semaphore_signal(barrier, inc=1, device_id=peer, device_id_type=pl.DeviceIdType.MESH)
    pl.semaphore_wait(barrier, len(peers))


def kernel(q, cent, stored, ids, home, probes, best, out, cent_in, stored_in, ids_in, high, low, base, pick, acc,
           partial, from_z, from_x, from_y, mid_z, mid_x, sends, recvs, local_sems):
    at, core = place()
    group = lax.axis_index("group")
    lists, places = ids.shape
    rows = lists * places
    cents = cent.shape[0]
    width = NY * NX * 8
    barrier, peers = greet(at, core)
    partner = device(at, 1 - core)
    meet(barrier, peers + [partner])
    used = [0]
    started = []

    def send(src, dst, to, sem):
        copy = pltpu.make_async_remote_copy(
            src_ref=src,
            dst_ref=dst,
            send_sem=sends.at[sem],
            recv_sem=recvs.at[sem],
            device_id=to,
            device_id_type=pl.DeviceIdType.MESH,
        )
        copy.start()
        return copy

    def arrived(slot, sem):
        pltpu.make_async_remote_copy(
            src_ref=slot,
            dst_ref=slot,
            send_sem=sends.at[sem],
            recv_sem=recvs.at[sem],
            device_id=partner,
            device_id_type=pl.DeviceIdType.MESH,
        ).wait_recv()

    def new_sem(count=1):
        used[0] += count
        return used[0] - count

    def columns(part):
        return q.at[:, pl.ds(part * PART, PART)]

    firsts = []
    for part, order in enumerate(ORDERS):
        mine = []
        for d in range(1, SIZES[order[0]]):
            sem = new_sem()
            slot = out.at[part, at[Z], at[Y], at[X]]
            started.append(send(columns(part), slot, device(moved(at, order[0], d), core), sem))
            fx, fy, fz = moved(at, order[0], -d)
            mine.append((out.at[part, fz, fy, fx], sem))
        firsts.append(mine)
    own = []
    for part in range(3):
        copy = pltpu.make_async_copy(columns(part), out.at[part, at[Z], at[Y], at[X]], local_sems.at[part])
        copy.start()
        own.append(copy)
    swaps = []
    for src, dst in ((stored, stored_in), (cent, cent_in), (ids, ids_in)):
        sem = new_sem()
        started.append(send(src, dst, partner, sem))
        swaps.append((dst, sem))

    def slab(part, phase, pos, half):
        x, y, z = at
        first = pl.ds(0 if half == 0 else (2 if (part, phase) == (0, 1) else 4), 2 if (part, phase) == (0, 1) else 4)
        if part == 0:
            return out.at[0, z, pos, first] if phase == 1 else out.at[0, pos, first]
        if part == 1:
            return out.at[1, pos, first, x] if phase == 1 else out.at[1, first, :, pos]
        return out.at[2, first, y, pos] if phase == 1 else out.at[2, first, pos]

    def ring(part, phase, filled=None):
        axis = ORDERS[part][phase]
        size = SIZES[axis]
        last = size // 2
        streams = []
        for way in (1, -1):
            for turn in (0, 1):
                half = turn if way == 1 else 1 - turn
                hops = last if turn == 0 else last - 1
                streams.append((way, turn, half, hops, [new_sem() for _ in range(hops)]))

        def pos(offset):
            return lax.rem(at[axis] + (offset + size), size)

        def hop(stream, step):
            way, turn, half, hops, sems = stream
            piece = slab(part, phase, pos(-way * step), half)
            started.append(send(piece, piece, device(moved(at, axis, way), core), sems[step]))

        def take(stream, step):
            way, turn, half, hops, sems = stream
            arrived(slab(part, phase, pos(-way * (step + 1)), half), sems[step])

        for turn in (0, 1):
            for stream in streams:
                if stream[1] == turn:
                    hop(stream, 0)
        if size == NX:
            yield
        for step in range(last):
            for turn in (0, 1):
                yield
                for stream in streams:
                    if stream[1] == turn and step < stream[3]:
                        take(stream, step)
                        if step + 1 < stream[3]:
                            hop(stream, step + 1)
            if filled is not None:
                filled(step)

    def dot(a, b):
        return lax.dot_general(a, b, (((1,), (1,)), ((), ())), preferred_element_type=jnp.float32)

    def product(part, z):
        rhs = out[part, z].reshape(width, PART)
        rhs_high = rhs.astype(jnp.bfloat16)
        rhs_low = (rhs - rhs_high.astype(jnp.float32)).astype(jnp.bfloat16)
        v_high = high[:, part * PART : (part + 1) * PART]
        v_low = low[:, part * PART : (part + 1) * PART]
        return dot(v_high, rhs_high) + (dot(v_high, rhs_low) + dot(v_low, rhs_high))

    def prepare_vectors():
        for slot, sem in swaps:
            arrived(slot, sem)
        start = 0
        for ref in (stored, stored_in, cent, cent_in):
            count = ref.shape[0]
            top = ref[...].astype(jnp.bfloat16)
            high[start : start + count, :] = top
            low[start : start + count, :] = (ref[...] - top.astype(jnp.float32)).astype(jnp.bfloat16)
            start += count
        across = lax.broadcasted_iota(jnp.int32, (places, places), 1)
        down = lax.broadcasted_iota(jnp.int32, (places, places), 0)
        for n, ref in enumerate((ids, ids_in)):
            for i in range(lists):
                row = jnp.where(ref[i : i + 1, :] >= 0, jnp.float32(0), jnp.float32(LOW))
                column = jnp.sum(jnp.where(across == down, row, jnp.float32(0)), axis=1, keepdims=True)
                first = n * rows + i * places
                base[first : first + places, :] = jnp.broadcast_to(column, (places, width))
        base[2 * rows :, :] = jnp.zeros((2 * cents, width), jnp.float32)

    def prepare_picks():
        at_slot = lax.broadcasted_iota(jnp.int32, home.shape, 1)
        row = lax.broadcasted_iota(jnp.int32, (probes.shape[0], width), 0)
        y_of = lax.broadcasted_iota(jnp.int32, (probes.shape[0], width), 1) // (NX * 8)
        for i in range(lists):
            held = jnp.max(jnp.where(home[...] == group * lists + i, at_slot, -1), axis=1, keepdims=True)
            hit = jnp.where(probes[...] == held, jnp.float32(0), jnp.float32(LOW))
            hit = jnp.max(hit, axis=1, keepdims=True)
            for zh in range(2):
                for s in range(STEPS):
                    here = row == (y_of * 2 + zh) * STEPS + s
                    line = jnp.where(here, hit, jnp.float32(LOW))
                    pick[zh, s * lists + i : s * lists + i + 1, :] = jnp.max(line, axis=0, keepdims=True)

    def first_third(begin, stride, count):
        def one(k, _):
            z = lax.rem(at[Z] + (begin + NZ + k * stride), NZ)
            acc[z] = base[...] + product(0, z)
            return 0

        lax.fori_loop(0, count, one, 0)

    def filled(step):
        if step == 0:
            first_third(-1, 1, 3)
        elif step < NZ // 2 - 1:
            first_third(-(step + 1), 2 * (step + 1), 2)
        else:
            first_third(NZ // 2, 1, 1)

    def whole(part):
        own[part].wait()
        for slot, sem in firsts[part]:
            arrived(slot, sem)
        yield from ring(part, 1)
        yield from ring(part, 2, filled if part == 0 else None)

    prepare_picks()
    running = [whole(0), whole(2), whole(1)]
    turns = 0
    while running:
        for item in list(running):
            try:
                next(item)
            except StopIteration:
                running.remove(item)
        turns += 1
        if turns == 4:
            prepare_vectors()

    first_z = new_sem(NZ)

    def z_copy(d):
        return pltpu.make_async_remote_copy(
            src_ref=partial.at[lax.rem(at[Z] + d, NZ)],
            dst_ref=from_z.at[d - 1],
            send_sem=sends.at[first_z + d],
            recv_sem=recvs.at[first_z + d],
            device_id=device(moved(at, Z, d), core),
            device_id_type=pl.DeviceIdType.MESH,
        )

    def distance(k):
        return NZ // 2 + ((k + 1) // 2) * (1 - 2 * (k % 2))

    def finish(k, _):
        @pl.when(k > 0)
        def _():
            z_copy(distance(k - 1)).start()

        z = lax.rem(at[Z] + distance(k), NZ)
        total = acc[z] + (product(1, z) + product(2, z))
        tops = []
        for i in range(lists):
            a = jnp.max(total[i * places : (i + 1) * places], axis=0, keepdims=True)
            b = jnp.max(total[rows + i * places : rows + (i + 1) * places], axis=0, keepdims=True)
            tops.append(jnp.maximum(a, b))
        partial[z, 0:1, :] = jnp.max(total[2 * rows :], axis=0, keepdims=True)
        chosen = pick[z // ZL]
        for s in range(STEPS):
            top = tops[0] + chosen[s * lists : s * lists + 1, :]
            for i in range(1, lists):
                top = jnp.maximum(top, tops[i] + chosen[s * lists + i : s * lists + i + 1, :])
            partial[z, s + 1 : s + 2, :] = top
        return 0

    lax.fori_loop(0, NZ, finish, 0)

    def most(value, landing):
        for i in range(landing.shape[0]):
            value = jnp.maximum(value, landing[i])
        return value

    def swap(axis, source, landing):
        copies = []
        for d in range(1, SIZES[axis]):
            copies.append(send(source, landing.at[d - 1], device(moved(at, axis, d), core), new_sem()))
        for copy in copies:
            copy.wait()

    for d in range(1, NZ):
        z_copy(d).wait()
    mid_z[...] = most(partial[at[Z]], from_z)
    swap(X, mid_z, from_x)
    mid_x[...] = most(mid_z[...], from_x)
    swap(Y, mid_x, from_y)
    best[...] = most(mid_x[...], from_y)
    for copy in started:
        copy.wait_send()


def local(queries, centroids, stored, vector_ids, list_home, probes):
    (x, y, z), core = place()
    lists, places = vector_ids.shape
    rows = lists * places
    cents = centroids.shape[0]
    f32 = jnp.float32
    width = NY * NX * 8
    piece = (1 + STEPS, width)
    held = 2 * rows + 2 * cents
    copies = 17 + 3 + 2 * 34 + NZ + NX + NY - 2
    best = pl.pallas_call(
        kernel,
        out_shape=jax.ShapeDtypeStruct(piece, f32),
        in_specs=[VMEM_SPEC] * 6,
        out_specs=VMEM_SPEC,
        scratch_shapes=[
            pltpu.VMEM((3, NZ, NY, NX, 8, PART), f32),
            pltpu.VMEM((cents, D), f32),
            pltpu.VMEM((rows, D), f32),
            pltpu.VMEM((lists, places), jnp.int32),
            pltpu.VMEM((held, D), jnp.bfloat16),
            pltpu.VMEM((held, D), jnp.bfloat16),
            pltpu.VMEM((held, width), f32),
            pltpu.VMEM((2, STEPS * lists, width), f32),
            pltpu.VMEM((NZ, held, width), f32),
            pltpu.VMEM((NZ,) + piece, f32),
            pltpu.VMEM((NZ - 1,) + piece, f32),
            pltpu.VMEM((NX - 1,) + piece, f32),
            pltpu.VMEM((NY - 1,) + piece, f32),
            pltpu.VMEM(piece, f32),
            pltpu.VMEM(piece, f32),
            pltpu.SemaphoreType.DMA((copies,)),
            pltpu.SemaphoreType.DMA((copies,)),
            pltpu.SemaphoreType.DMA((3,)),
        ],
        compiler_params=pltpu.CompilerParams(collective_id=0, has_side_effects=True, vmem_limit_bytes=48 << 20),
        name="search",
    )(queries, centroids, stored.reshape(rows, D), vector_ids, list_home.reshape(1, -1), probes.reshape(-1, probes.shape[2]))
    mine = lax.dynamic_slice_in_dim(best, (y * NX + x) * 8, 8, 1)
    return mine[0], mine[1:]


def solution(mesh):
    placed = (
        P(AXES, None),
        P(AXES, None),
        P("group", "member", None),
        P("group", "member"),
        P(),
        P(),
    )
    return jax.shard_map(
        local,
        mesh=mesh,
        in_specs=placed,
        out_specs=(P(AXES), P(None, AXES)),
        check_vma=False,
    )
```

```python
import heapq

import jax
import jax.numpy as jnp
from jax import lax
from jax.experimental import pallas as pl
from jax.experimental.pallas import tpu as pltpu
from jax.sharding import PartitionSpec as P

D = 768
STEPS = 3
AXES = ("group", "member")
LOW = -1e30
NX, NY, NZ, ZL = 4, 8, 8, 4
PART = D // 3
SIZES = (NX, NY, NZ)
X, Y, Z = 0, 1, 2
ORDERS = ((Y, X, Z), (Y, Z, X), (Z, X, Y))
RATE, HOP, START = 46000.0, 0.8, 0.9
VMEM_SPEC = pl.BlockSpec(memory_space=pltpu.VMEM)


def place():
    g, m = lax.axis_index("group"), lax.axis_index("member")
    x, y, core = (m // 2) % NX, g // 2, m % 2
    z = (g % 2) * ZL + m // (2 * NX)
    return [x, y, z], core


def device(at, core):
    x, y, z = at
    return (y * 2 + z // ZL, (z % ZL) * (2 * NX) + x * 2 + core)


def moved(at, axis, steps):
    size = SIZES[axis]
    out = list(at)
    out[axis] = lax.rem(at[axis] + (steps + size), size)
    return out


def greet(at, core):
    barrier = pltpu.get_barrier_semaphore()
    peers = [device(moved(at, axis, d), core) for axis in (X, Y, Z) for d in range(1, SIZES[axis])]
    return barrier, peers


def meet(barrier, peers):
    for peer in peers:
        pl.semaphore_signal(barrier, inc=1, device_id=peer, device_id_type=pl.DeviceIdType.MESH)
    pl.semaphore_wait(barrier, len(peers))


def kernel(q, cent_hbm, stored_hbm, ids_hbm, home_hbm, probes_hbm, best, out, cent, stored, ids, home, probes, cent_in, stored_in, ids_in, high, low, base, pick, acc,
           partial, from_z, from_x, from_y, mid_z, mid_x, sends, recvs, local_sems):
    at, core = place()
    group = lax.axis_index("group")
    lists, places = ids.shape
    rows = lists * places
    cents = cent.shape[0]
    width = NY * NX * 8
    barrier, peers = greet(at, core)
    partner = device(at, 1 - core)
    meet(barrier, peers + [partner])
    used = [0]
    started = []

    def send(src, dst, to, sem):
        copy = pltpu.make_async_remote_copy(
            src_ref=src,
            dst_ref=dst,
            send_sem=sends.at[sem],
            recv_sem=recvs.at[sem],
            device_id=to,
            device_id_type=pl.DeviceIdType.MESH,
        )
        copy.start()
        return copy

    def arrived(slot, sem):
        pltpu.make_async_remote_copy(
            src_ref=slot,
            dst_ref=slot,
            send_sem=sends.at[sem],
            recv_sem=recvs.at[sem],
            device_id=partner,
            device_id_type=pl.DeviceIdType.MESH,
        ).wait_recv()

    def new_sem(count=1):
        used[0] += count
        return used[0] - count

    def columns(part):
        return q.at[:, pl.ds(part * PART, PART)]

    own = []
    for part in range(3):
        own.append(pltpu.make_async_copy(columns(part), out.at[part, at[Z], at[Y], at[X]], local_sems.at[part]))
    loads = [
        pltpu.make_async_copy(stored_hbm, stored, local_sems.at[3]),
        pltpu.make_async_copy(cent_hbm, cent, local_sems.at[4]),
        pltpu.make_async_copy(ids_hbm, ids, local_sems.at[5]),
    ]

    tables = [
        pltpu.make_async_copy(home_hbm, home, local_sems.at[6]),
        pltpu.make_async_copy(probes_hbm, probes, local_sems.at[7]),
    ]

    events = []
    free = {}
    count = [0]

    def at_time(when, action):
        count[0] += 1
        heapq.heappush(events, (when, count[0], action))

    def link(now, axis, way, size):
        done = max(now, free.get((axis, way), 0.0)) + size / RATE
        free[axis, way] = done
        return done + HOP + START

    def index(axis, offset):
        return lax.rem(at[axis] + (offset + SIZES[axis]), SIZES[axis])

    def chunk(part, b, c, half=None):
        span = slice(None) if half is None else pl.ds(4 * half, 4)
        if part == 0:
            return out.at[0, c, span, b]
        if part == 1:
            return out.at[1, b, span, c]
        return out.at[2, span, c, b]

    chunk_bytes = 8 * 8 * PART * 4
    left = {}
    swaps = []

    def run_part(part):
        first, second, third = ORDERS[part]
        turns = [0]
        for d in range(1, SIZES[second] // 2):
            turns += [-d, d]
        turns.append(SIZES[second] // 2)

        def last_hop(b_off, way, step, now):
            if step == SIZES[third] // 2 and (turns.index(b_off) % 2 == 0) != (way == 1):
                return
            sem = new_sem()
            piece = chunk(part, index(second, b_off), index(third, -way * (step - 1)))
            started.append(send(piece, piece, device(moved(at, third, way), core), sem))

            def take(when):
                arrived(chunk(part, index(second, b_off), index(third, -way * step)), sem)
                if step < SIZES[third] // 2:
                    last_hop(b_off, way, step + 1, when)
                left[part, step] -= 1
                if part == 0 and left[part, step] == 0:
                    filled(step - 1)

            at_time(link(now, third, way, chunk_bytes), take)

        def have(b_off, now):
            for way in (1, -1):
                last_hop(b_off, way, 1, now)

        def middle_hop(way, step, now):
            last = step == SIZES[second] // 2
            half = None if not last else (0 if way == 1 else 1)
            sem = new_sem()
            piece = chunk(part, index(second, -way * (step - 1)), at[third], half)
            started.append(send(piece, piece, device(moved(at, second, way), core), sem))

            def take(when):
                arrived(chunk(part, index(second, -way * step), at[third], half), sem)
                if not last:
                    middle_hop(way, step + 1, when)
                    have(-way * step, when)
                else:
                    left[part, "middle"] -= 1
                    if left[part, "middle"] == 0:
                        have(step, when)

            at_time(link(now, second, way, chunk_bytes // 2 if last else chunk_bytes), take)

        left[part, "middle"] = 2
        for step in range(1, SIZES[third] // 2 + 1):
            left[part, step] = SIZES[second] * (1 if step == SIZES[third] // 2 else 2)

        mine = []
        for d in range(1, SIZES[first]):
            sem = new_sem()
            slot = out.at[part, at[Z], at[Y], at[X]]
            started.append(send(columns(part), slot, device(moved(at, first, d), core), sem))
            fx, fy, fz = moved(at, first, -d)
            mine.append((out.at[part, fz, fy, fx], sem))

        def take(when):
            own[part].wait()
            for slot, sem in mine:
                arrived(slot, sem)
            for way in (1, -1):
                middle_hop(way, 1, when)
            have(0, when)

        at_time(START + HOP * SIZES[first] // 2 + 0.001 * part, take)

    def dot(a, b):
        return lax.dot_general(a, b, (((1,), (1,)), ((), ())), preferred_element_type=jnp.float32)

    def product(part, z):
        rhs = out[part, z].reshape(width, PART)
        rhs_high = rhs.astype(jnp.bfloat16)
        rhs_low = (rhs - rhs_high.astype(jnp.float32)).astype(jnp.bfloat16)
        v_high = high[:, part * PART : (part + 1) * PART]
        v_low = low[:, part * PART : (part + 1) * PART]
        return dot(v_high, rhs_high) + (dot(v_high, rhs_low) + dot(v_low, rhs_high))

    def prepare_vectors(when):
        for copy in loads:
            copy.wait()
        for slot, sem in swaps:
            arrived(slot, sem)
        start = 0
        for ref in (stored, stored_in, cent, cent_in):
            count = ref.shape[0]
            top = ref[...].astype(jnp.bfloat16)
            high[start : start + count, :] = top
            low[start : start + count, :] = (ref[...] - top.astype(jnp.float32)).astype(jnp.bfloat16)
            start += count
        across = lax.broadcasted_iota(jnp.int32, (places, places), 1)
        down = lax.broadcasted_iota(jnp.int32, (places, places), 0)
        for n, ref in enumerate((ids, ids_in)):
            for i in range(lists):
                row = jnp.where(ref[i : i + 1, :] >= 0, jnp.float32(0), jnp.float32(LOW))
                column = jnp.sum(jnp.where(across == down, row, jnp.float32(0)), axis=1, keepdims=True)
                first = n * rows + i * places
                base[first : first + places, :] = jnp.broadcast_to(column, (places, width))
        base[2 * rows :, :] = jnp.zeros((2 * cents, width), jnp.float32)

    def prepare_picks():
        for copy in tables:
            copy.wait()
        at_slot = lax.broadcasted_iota(jnp.int32, home.shape, 1)
        row = lax.broadcasted_iota(jnp.int32, (probes.shape[1], width), 0)
        y_of = lax.broadcasted_iota(jnp.int32, (probes.shape[1], width), 1) // (NX * 8)
        for i in range(lists):
            held = jnp.max(jnp.where(home[...] == group * lists + i, at_slot, -1), axis=1, keepdims=True)
            for s in range(STEPS):
                hit = jnp.where(probes[s] == held, jnp.float32(0), jnp.float32(LOW))
                hit = jnp.max(hit, axis=1, keepdims=True)
                for zh in range(2):
                    line = jnp.where(row == y_of * 2 + zh, hit, jnp.float32(LOW))
                    pick[zh, s * lists + i : s * lists + i + 1, :] = jnp.max(line, axis=0, keepdims=True)

    def first_third(begin, stride, count):
        def one(k, _):
            z = lax.rem(at[Z] + (begin + NZ + k * stride), NZ)
            acc[z] = base[...] + product(0, z)
            return 0

        lax.fori_loop(0, count, one, 0)

    def filled(step):
        if step == 0:
            first_third(-1, 1, 3)
        elif step < NZ // 2 - 1:
            first_third(-(step + 1), 2 * (step + 1), 2)
        else:
            first_third(NZ // 2, 1, 1)

    for part in (1, 2, 0):
        run_part(part)
    for copy in own + tables + loads:
        copy.start()
    for src, dst in ((stored_hbm, stored_in), (cent_hbm, cent_in), (ids_hbm, ids_in)):
        sem = new_sem()
        started.append(send(src, dst, partner, sem))
        swaps.append((dst, sem))
    prepare_picks()
    at_time(9.0, prepare_vectors)
    while events:
        when, _, action = heapq.heappop(events)
        action(when)

    first_z = new_sem(NZ)

    def z_copy(d):
        return pltpu.make_async_remote_copy(
            src_ref=partial.at[lax.rem(at[Z] + d, NZ)],
            dst_ref=from_z.at[d - 1],
            send_sem=sends.at[first_z + d],
            recv_sem=recvs.at[first_z + d],
            device_id=device(moved(at, Z, d), core),
            device_id_type=pl.DeviceIdType.MESH,
        )

    def distance(k):
        return NZ // 2 + ((k + 1) // 2) * (1 - 2 * (k % 2))

    def finish(k, _):
        @pl.when(k > 0)
        def _():
            z_copy(distance(k - 1)).start()

        z = lax.rem(at[Z] + distance(k), NZ)
        total = acc[z] + (product(1, z) + product(2, z))
        tops = []
        for i in range(lists):
            a = jnp.max(total[i * places : (i + 1) * places], axis=0, keepdims=True)
            b = jnp.max(total[rows + i * places : rows + (i + 1) * places], axis=0, keepdims=True)
            tops.append(jnp.maximum(a, b))
        partial[z, 0:1, :] = jnp.max(total[2 * rows :], axis=0, keepdims=True)
        chosen = pick[z // ZL]
        for s in range(STEPS):
            top = tops[0] + chosen[s * lists : s * lists + 1, :]
            for i in range(1, lists):
                top = jnp.maximum(top, tops[i] + chosen[s * lists + i : s * lists + i + 1, :])
            partial[z, s + 1 : s + 2, :] = top
        return 0

    lax.fori_loop(0, NZ, finish, 0)

    def most(value, landing):
        for i in range(landing.shape[0]):
            value = jnp.maximum(value, landing[i])
        return value

    def swap(axis, source, landing):
        copies = []
        for d in range(1, SIZES[axis]):
            copies.append(send(source, landing.at[d - 1], device(moved(at, axis, d), core), new_sem()))
        for copy in copies:
            copy.wait()

    for d in range(1, NZ):
        z_copy(d).wait()
    mid_z[...] = most(partial[at[Z]], from_z)
    swap(X, mid_z, from_x)
    mid_x[...] = most(mid_z[...], from_x)
    swap(Y, mid_x, from_y)
    best[...] = most(mid_x[...], from_y)
    for copy in started:
        copy.wait_send()


def local(queries, centroids, stored, vector_ids, list_home, probes):
    (x, y, z), core = place()
    lists, places = vector_ids.shape
    rows = lists * places
    cents = centroids.shape[0]
    f32 = jnp.float32
    width = NY * NX * 8
    piece = (1 + STEPS, width)
    held = 2 * rows + 2 * cents
    copies = 21 + 3 + 16 + 80 + NZ + NX + NY - 2
    best = pl.pallas_call(
        kernel,
        out_shape=jax.ShapeDtypeStruct(piece, f32),
        in_specs=[pl.BlockSpec(memory_space=pltpu.HBM)] * 6,
        out_specs=VMEM_SPEC,
        scratch_shapes=[
            pltpu.VMEM((3, NZ, NY, NX, 8, PART), f32),
            pltpu.VMEM((cents, D), f32),
            pltpu.VMEM((rows, D), f32),
            pltpu.VMEM((lists, places), jnp.int32),
            pltpu.VMEM((1, list_home.shape[0]), jnp.int32),
            pltpu.VMEM((STEPS, probes.shape[0], probes.shape[2]), jnp.int32),
            pltpu.VMEM((cents, D), f32),
            pltpu.VMEM((rows, D), f32),
            pltpu.VMEM((lists, places), jnp.int32),
            pltpu.VMEM((held, D), jnp.bfloat16),
            pltpu.VMEM((held, D), jnp.bfloat16),
            pltpu.VMEM((held, width), f32),
            pltpu.VMEM((2, STEPS * lists, width), f32),
            pltpu.VMEM((NZ, held, width), f32),
            pltpu.VMEM((NZ,) + piece, f32),
            pltpu.VMEM((NZ - 1,) + piece, f32),
            pltpu.VMEM((NX - 1,) + piece, f32),
            pltpu.VMEM((NY - 1,) + piece, f32),
            pltpu.VMEM(piece, f32),
            pltpu.VMEM(piece, f32),
            pltpu.SemaphoreType.DMA((copies,)),
            pltpu.SemaphoreType.DMA((copies,)),
            pltpu.SemaphoreType.DMA((8,)),
        ],
        compiler_params=pltpu.CompilerParams(collective_id=0, has_side_effects=True, vmem_limit_bytes=66_900_000),
        name="search",
    )(queries, centroids, stored.reshape(rows, D), vector_ids, list_home.reshape(1, -1), jnp.transpose(probes, (1, 0, 2)))
    mine = lax.dynamic_slice_in_dim(best, (y * NX + x) * 8, 8, 1)
    return mine[0], mine[1:]


def solution(mesh):
    placed = (
        P(AXES, None),
        P(AXES, None),
        P("group", "member", None),
        P("group", "member"),
        P(),
        P(),
    )
    return jax.shard_map(
        local,
        mesh=mesh,
        in_specs=placed,
        out_specs=(P(AXES), P(None, AXES)),
        check_vma=False,
    )
```

```python
import heapq

import jax
import jax.numpy as jnp
from jax import lax
from jax.experimental import pallas as pl
from jax.experimental.pallas import tpu as pltpu
from jax.sharding import PartitionSpec as P

D = 768
STEPS = 3
AXES = ("group", "member")
LOW = -1e30
NX, NY, NZ, ZL = 4, 8, 8, 4
PART = D // 3
SIZES = (NX, NY, NZ)
X, Y, Z = 0, 1, 2
ORDERS = ((Y, X, Z), (Y, Z, X), (Z, X, Y))
RATE, HOP, START = 36000.0, 0.8, 0.9
VMEM_SPEC = pl.BlockSpec(memory_space=pltpu.VMEM)


def place():
    g, m = lax.axis_index("group"), lax.axis_index("member")
    x, y, core = (m // 2) % NX, g // 2, m % 2
    z = (g % 2) * ZL + m // (2 * NX)
    return [x, y, z], core


def device(at, core):
    x, y, z = at
    return (y * 2 + z // ZL, (z % ZL) * (2 * NX) + x * 2 + core)


def moved(at, axis, steps):
    size = SIZES[axis]
    out = list(at)
    out[axis] = lax.rem(at[axis] + (steps + size), size)
    return out


def greet(at, core):
    barrier = pltpu.get_barrier_semaphore()
    peers = [device(moved(at, axis, d), core) for axis in (X, Y, Z) for d in range(1, SIZES[axis])]
    return barrier, peers


def meet(barrier, peers):
    for peer in peers:
        pl.semaphore_signal(barrier, inc=1, device_id=peer, device_id_type=pl.DeviceIdType.MESH)
    pl.semaphore_wait(barrier, len(peers))


def kernel(q, cent_hbm, stored_hbm, ids_hbm, home_hbm, probes_hbm, best, out, cent, stored, ids, home, probes, cent_in, stored_in, ids_in, high, low, base, pick, acc,
           partial, from_z, from_x, from_y, mid_z, mid_x, sends, recvs, local_sems):
    at, core = place()
    group = lax.axis_index("group")
    lists, places = ids.shape
    rows = lists * places
    cents = cent.shape[0]
    width = NY * NX * 8
    barrier, peers = greet(at, core)
    partner = device(at, 1 - core)
    meet(barrier, peers + [partner])
    used = [0]
    started = []

    def send(src, dst, to, sem):
        copy = pltpu.make_async_remote_copy(
            src_ref=src,
            dst_ref=dst,
            send_sem=sends.at[sem],
            recv_sem=recvs.at[sem],
            device_id=to,
            device_id_type=pl.DeviceIdType.MESH,
        )
        copy.start()
        return copy

    def arrived(slot, sem):
        pltpu.make_async_remote_copy(
            src_ref=slot,
            dst_ref=slot,
            send_sem=sends.at[sem],
            recv_sem=recvs.at[sem],
            device_id=partner,
            device_id_type=pl.DeviceIdType.MESH,
        ).wait_recv()

    def new_sem(count=1):
        used[0] += count
        return used[0] - count

    def columns(part):
        return q.at[:, pl.ds(part * PART, PART)]

    own = []
    for part in range(3):
        own.append(pltpu.make_async_copy(columns(part), out.at[part, at[Z], at[Y], at[X]], local_sems.at[part]))
    loads = [
        pltpu.make_async_copy(stored_hbm, stored, local_sems.at[3]),
        pltpu.make_async_copy(cent_hbm, cent, local_sems.at[4]),
        pltpu.make_async_copy(ids_hbm, ids, local_sems.at[5]),
    ]

    tables = [
        pltpu.make_async_copy(home_hbm, home, local_sems.at[6]),
        pltpu.make_async_copy(probes_hbm, probes, local_sems.at[7]),
    ]

    events = []
    free = {}
    count = [0]

    def at_time(when, action):
        count[0] += 1
        heapq.heappush(events, (when, count[0], action))

    def link(now, axis, way, size):
        done = max(now, free.get((axis, way), 0.0)) + size / RATE
        free[axis, way] = done
        return done + HOP + START

    def index(axis, offset):
        return lax.rem(at[axis] + (offset + SIZES[axis]), SIZES[axis])

    def chunk(part, b, c, half=None):
        span = slice(None) if half is None else pl.ds(4 * half, 4)
        if part == 0:
            return out.at[0, c, span, b]
        if part == 1:
            return out.at[1, b, span, c]
        return out.at[2, span, c, b]

    chunk_bytes = 8 * 8 * PART * 4
    left = {}
    swaps = []

    def run_part(part):
        first, second, third = ORDERS[part]
        turns = [0]
        for d in range(1, SIZES[second] // 2):
            turns += [-d, d]
        turns.append(SIZES[second] // 2)

        def last_hop(b_off, way, step, now):
            if step == SIZES[third] // 2 and (turns.index(b_off) % 2 == 0) != (way == 1):
                return
            sem = new_sem()
            piece = chunk(part, index(second, b_off), index(third, -way * (step - 1)))
            started.append(send(piece, piece, device(moved(at, third, way), core), sem))

            def take(when):
                arrived(chunk(part, index(second, b_off), index(third, -way * step)), sem)
                if step < SIZES[third] // 2:
                    last_hop(b_off, way, step + 1, when)
                left[part, step] -= 1
                if left[part, step] == 0:
                    filled(part, step, when)

            at_time(link(now, third, way, chunk_bytes), take)

        def have(b_off, now):
            for way in (1, -1):
                last_hop(b_off, way, 1, now)

        def middle_hop(way, step, now):
            last = step == SIZES[second] // 2
            half = None if not last else (0 if way == 1 else 1)
            sem = new_sem()
            piece = chunk(part, index(second, -way * (step - 1)), at[third], half)
            started.append(send(piece, piece, device(moved(at, second, way), core), sem))

            def take(when):
                arrived(chunk(part, index(second, -way * step), at[third], half), sem)
                if not last:
                    middle_hop(way, step + 1, when)
                    have(-way * step, when)
                else:
                    left[part, "middle"] -= 1
                    if left[part, "middle"] == 0:
                        have(step, when)

            at_time(link(now, second, way, chunk_bytes // 2 if last else chunk_bytes), take)

        left[part, "middle"] = 2
        for step in range(1, SIZES[third] // 2 + 1):
            left[part, step] = SIZES[second] * (1 if step == SIZES[third] // 2 else 2)

        mine = []
        for d in range(1, SIZES[first]):
            sem = new_sem()
            slot = out.at[part, at[Z], at[Y], at[X]]
            started.append(send(columns(part), slot, device(moved(at, first, d), core), sem))
            fx, fy, fz = moved(at, first, -d)
            mine.append((out.at[part, fz, fy, fx], sem))

        def take(when):
            own[part].wait()
            for slot, sem in mine:
                arrived(slot, sem)
            for way in (1, -1):
                middle_hop(way, 1, when)
            have(0, when)

        at_time(START + HOP * SIZES[first] // 2 + 0.001 * part, take)

    def dot(a, b):
        return lax.dot_general(a, b, (((1,), (1,)), ((), ())), preferred_element_type=jnp.float32)

    def product(part, z):
        rhs = out[part, z].reshape(width, PART)
        rhs_high = rhs.astype(jnp.bfloat16)
        rhs_low = (rhs - rhs_high.astype(jnp.float32)).astype(jnp.bfloat16)
        v_high = high[:, part * PART : (part + 1) * PART]
        v_low = low[:, part * PART : (part + 1) * PART]
        return dot(v_high, rhs_high) + (dot(v_high, rhs_low) + dot(v_low, rhs_high))

    def prepare_vectors(when):
        for copy in loads:
            copy.wait()
        for slot, sem in swaps:
            arrived(slot, sem)
        start = 0
        for ref in (stored, stored_in, cent, cent_in):
            count = ref.shape[0]
            top = ref[...].astype(jnp.bfloat16)
            high[start : start + count, :] = top
            low[start : start + count, :] = (ref[...] - top.astype(jnp.float32)).astype(jnp.bfloat16)
            start += count
        across = lax.broadcasted_iota(jnp.int32, (places, places), 1)
        down = lax.broadcasted_iota(jnp.int32, (places, places), 0)
        for n, ref in enumerate((ids, ids_in)):
            for i in range(lists):
                row = jnp.where(ref[i : i + 1, :] >= 0, jnp.float32(0), jnp.float32(LOW))
                column = jnp.sum(jnp.where(across == down, row, jnp.float32(0)), axis=1, keepdims=True)
                first = n * rows + i * places
                base[first : first + places, :] = jnp.broadcast_to(column, (places, width))
        base[2 * rows :, :] = jnp.zeros((2 * cents, width), jnp.float32)

        def fill(z, _):
            acc[z] = base[...]
            return 0

        lax.fori_loop(0, NZ, fill, 0)

    def prepare_picks():
        for copy in tables:
            copy.wait()
        at_slot = lax.broadcasted_iota(jnp.int32, home.shape, 1)
        row = lax.broadcasted_iota(jnp.int32, (probes.shape[1], width), 0)
        y_of = lax.broadcasted_iota(jnp.int32, (probes.shape[1], width), 1) // (NX * 8)
        for i in range(lists):
            held = jnp.max(jnp.where(home[...] == group * lists + i, at_slot, -1), axis=1, keepdims=True)
            for s in range(STEPS):
                hit = jnp.where(probes[s] == held, jnp.float32(0), jnp.float32(LOW))
                hit = jnp.max(hit, axis=1, keepdims=True)
                for zh in range(2):
                    line = jnp.where(row == y_of * 2 + zh, hit, jnp.float32(LOW))
                    pick[zh, s * lists + i : s * lists + i + 1, :] = jnp.max(line, axis=0, keepdims=True)

    def add_products(part, begin, stride, count):
        def one(k, _):
            z = lax.rem(at[Z] + (begin + NZ + k * stride), NZ)
            acc[z] += product(part, z)
            return 0

        lax.fori_loop(0, count, one, 0)

    def filled(part, step, when):
        if part == 0:
            if step == 1:
                add_products(0, -1, 1, 3)
            elif step < NZ // 2:
                add_products(0, -step, 2 * step, 2)
            else:
                add_products(0, NZ // 2, 1, 1)
        elif all(left[part, n] == 0 for n in range(1, SIZES[ORDERS[part][2]] // 2 + 1)):
            for n in range(0, NZ, 2):
                at_time(when + 0.4 * n, lambda _, n=n: add_products(part, n, 1, 2))

    for part in (1, 2, 0):
        run_part(part)
    for copy in own + tables + loads:
        copy.start()
    for src, dst in ((stored_hbm, stored_in), (cent_hbm, cent_in), (ids_hbm, ids_in)):
        sem = new_sem()
        started.append(send(src, dst, partner, sem))
        swaps.append((dst, sem))
    prepare_picks()
    at_time(9.0, prepare_vectors)
    while events:
        when, _, action = heapq.heappop(events)
        action(when)

    first_z = new_sem(NZ)

    def z_copy(d):
        return pltpu.make_async_remote_copy(
            src_ref=partial.at[lax.rem(at[Z] + d, NZ)],
            dst_ref=from_z.at[d - 1],
            send_sem=sends.at[first_z + d],
            recv_sem=recvs.at[first_z + d],
            device_id=device(moved(at, Z, d), core),
            device_id_type=pl.DeviceIdType.MESH,
        )

    def distance(k):
        return NZ // 2 + ((k + 1) // 2) * (1 - 2 * (k % 2))

    def finish(k, _):
        @pl.when(k > 0)
        def _():
            z_copy(distance(k - 1)).start()

        z = lax.rem(at[Z] + distance(k), NZ)
        total = acc.at[z]
        tops = []
        for i in range(lists):
            a = jnp.max(total[i * places : (i + 1) * places, :], axis=0, keepdims=True)
            b = jnp.max(total[rows + i * places : rows + (i + 1) * places, :], axis=0, keepdims=True)
            tops.append(jnp.maximum(a, b))
        partial[z, 0:1, :] = jnp.max(total[2 * rows :, :], axis=0, keepdims=True)
        chosen = pick[z // ZL]
        for s in range(STEPS):
            top = tops[0] + chosen[s * lists : s * lists + 1, :]
            for i in range(1, lists):
                top = jnp.maximum(top, tops[i] + chosen[s * lists + i : s * lists + i + 1, :])
            partial[z, s + 1 : s + 2, :] = top
        return 0

    lax.fori_loop(0, NZ, finish, 0)

    def most(value, landing):
        for i in range(landing.shape[0]):
            value = jnp.maximum(value, landing[i])
        return value

    def swap(axis, source, landing):
        copies = []
        for d in range(1, SIZES[axis]):
            copies.append(send(source, landing.at[d - 1], device(moved(at, axis, d), core), new_sem()))
        for copy in copies:
            copy.wait()

    for d in range(1, NZ):
        z_copy(d).wait()
    mid_z[...] = most(partial[at[Z]], from_z)
    swap(X, mid_z, from_x)
    mid_x[...] = most(mid_z[...], from_x)
    swap(Y, mid_x, from_y)
    best[...] = most(mid_x[...], from_y)
    for copy in started:
        copy.wait_send()


def local(queries, centroids, stored, vector_ids, list_home, probes):
    (x, y, z), core = place()
    lists, places = vector_ids.shape
    rows = lists * places
    cents = centroids.shape[0]
    f32 = jnp.float32
    width = NY * NX * 8
    piece = (1 + STEPS, width)
    held = 2 * rows + 2 * cents
    copies = 21 + 3 + 16 + 80 + NZ + NX + NY - 2
    best = pl.pallas_call(
        kernel,
        out_shape=jax.ShapeDtypeStruct(piece, f32),
        in_specs=[pl.BlockSpec(memory_space=pltpu.HBM)] * 6,
        out_specs=VMEM_SPEC,
        scratch_shapes=[
            pltpu.VMEM((3, NZ, NY, NX, 8, PART), f32),
            pltpu.VMEM((cents, D), f32),
            pltpu.VMEM((rows, D), f32),
            pltpu.VMEM((lists, places), jnp.int32),
            pltpu.VMEM((1, list_home.shape[0]), jnp.int32),
            pltpu.VMEM((STEPS, probes.shape[0], probes.shape[2]), jnp.int32),
            pltpu.VMEM((cents, D), f32),
            pltpu.VMEM((rows, D), f32),
            pltpu.VMEM((lists, places), jnp.int32),
            pltpu.VMEM((held, D), jnp.bfloat16),
            pltpu.VMEM((held, D), jnp.bfloat16),
            pltpu.VMEM((held, width), f32),
            pltpu.VMEM((2, STEPS * lists, width), f32),
            pltpu.VMEM((NZ, held, width), f32),
            pltpu.VMEM((NZ,) + piece, f32),
            pltpu.VMEM((NZ - 1,) + piece, f32),
            pltpu.VMEM((NX - 1,) + piece, f32),
            pltpu.VMEM((NY - 1,) + piece, f32),
            pltpu.VMEM(piece, f32),
            pltpu.VMEM(piece, f32),
            pltpu.SemaphoreType.DMA((copies,)),
            pltpu.SemaphoreType.DMA((copies,)),
            pltpu.SemaphoreType.DMA((8,)),
        ],
        compiler_params=pltpu.CompilerParams(collective_id=0, has_side_effects=True, vmem_limit_bytes=66_900_000),
        name="search",
    )(queries, centroids, stored.reshape(rows, D), vector_ids, list_home.reshape(1, -1), jnp.transpose(probes, (1, 0, 2)))
    mine = lax.dynamic_slice_in_dim(best, (y * NX + x) * 8, 8, 1)
    return mine[0], mine[1:]


def solution(mesh):
    placed = (
        P(AXES, None),
        P(AXES, None),
        P("group", "member", None),
        P("group", "member"),
        P(),
        P(),
    )
    return jax.shard_map(
        local,
        mesh=mesh,
        in_specs=placed,
        out_specs=(P(AXES), P(None, AXES)),
        check_vma=False,
    )
```

```python
import heapq

import jax
import jax.numpy as jnp
from jax import lax
from jax.experimental import pallas as pl
from jax.experimental.pallas import tpu as pltpu
from jax.sharding import PartitionSpec as P

D = 768
STEPS = 3
AXES = ("group", "member")
LOW = -1e30
NX, NY, NZ, ZL = 4, 8, 8, 4
PART = D // 3
SIZES = (NX, NY, NZ)
X, Y, Z = 0, 1, 2
ORDERS = ((Y, X, Z), (Y, Z, X), (Z, X, Y))
RATE, HOP, START = 36000.0, 0.8, 0.9
VMEM_SPEC = pl.BlockSpec(memory_space=pltpu.VMEM)


def place():
    g, m = lax.axis_index("group"), lax.axis_index("member")
    x, y, core = (m // 2) % NX, g // 2, m % 2
    z = (g % 2) * ZL + m // (2 * NX)
    return [x, y, z], core


def device(at, core):
    x, y, z = at
    return (y * 2 + z // ZL, (z % ZL) * (2 * NX) + x * 2 + core)


def moved(at, axis, steps):
    size = SIZES[axis]
    out = list(at)
    out[axis] = lax.rem(at[axis] + (steps + size), size)
    return out


def greet(at, core):
    barrier = pltpu.get_barrier_semaphore()
    peers = [device(moved(at, axis, d), core) for axis in (X, Y, Z) for d in range(1, SIZES[axis])]
    return barrier, peers


def meet(barrier, peers):
    for peer in peers:
        pl.semaphore_signal(barrier, inc=1, device_id=peer, device_id_type=pl.DeviceIdType.MESH)
    pl.semaphore_wait(barrier, len(peers))


def kernel(q, cent_hbm, stored_hbm, ids_hbm, home_hbm, probes_hbm, best, out, out_z, cent, stored, ids, home, probes, cent_in, stored_in, ids_in, high, low, base, pick, acc,
           partial, from_z, from_x, from_y, mid_z, mid_x, sends, recvs, local_sems):
    at, core = place()
    group = lax.axis_index("group")
    lists, places = ids.shape
    rows = lists * places
    cents = cent.shape[0]
    width = NY * NX * 8
    barrier, peers = greet(at, core)
    partner = device(at, 1 - core)
    meet(barrier, peers + [partner])
    used = [0]
    started = []

    def send(src, dst, to, sem):
        copy = pltpu.make_async_remote_copy(
            src_ref=src,
            dst_ref=dst,
            send_sem=sends.at[sem],
            recv_sem=recvs.at[sem],
            device_id=to,
            device_id_type=pl.DeviceIdType.MESH,
        )
        copy.start()
        return copy

    def arrived(slot, sem):
        pltpu.make_async_remote_copy(
            src_ref=slot,
            dst_ref=slot,
            send_sem=sends.at[sem],
            recv_sem=recvs.at[sem],
            device_id=partner,
            device_id_type=pl.DeviceIdType.MESH,
        ).wait_recv()

    def new_sem(count=1):
        used[0] += count
        return used[0] - count

    def columns(part):
        return q.at[:, pl.ds(part * PART, PART)]

    def rows_of(part, x, y, z):
        return out_z.at[x, y, z] if part == 2 else out.at[part, z, x, y]

    own = []
    for part in range(3):
        own.append(pltpu.make_async_copy(columns(part), rows_of(part, *at), local_sems.at[part]))
    loads = [
        pltpu.make_async_copy(stored_hbm, stored, local_sems.at[3]),
        pltpu.make_async_copy(cent_hbm, cent, local_sems.at[4]),
        pltpu.make_async_copy(ids_hbm, ids, local_sems.at[5]),
    ]

    tables = [
        pltpu.make_async_copy(home_hbm, home, local_sems.at[6]),
        pltpu.make_async_copy(probes_hbm, probes, local_sems.at[7]),
    ]

    events = []
    free = {}
    count = [0]

    def at_time(when, action):
        count[0] += 1
        heapq.heappush(events, (when, count[0], action))

    def link(now, axis, way, size):
        done = max(now, free.get((axis, way), 0.0)) + size / RATE
        free[axis, way] = done
        return done + HOP + START

    def index(axis, offset):
        return lax.rem(at[axis] + (offset + SIZES[axis]), SIZES[axis])

    def chunk(part, b, c, half=None):
        span = slice(None) if half is None else pl.ds(4 * half, 4)
        if part == 0:
            return out.at[0, c, b, span]
        if part == 1:
            return out.at[1, b, c, span]
        return out_z.at[b, c, span]

    chunk_bytes = 8 * 8 * PART * 4
    left = {}
    swaps = []
    later = [lambda: prepare_vectors()]
    copies = 21 + 3 + 16 + 80

    def run_part(part):
        first, second, third = ORDERS[part]
        turns = [0]
        for d in range(1, SIZES[second] // 2):
            turns += [-d, d]
        turns.append(SIZES[second] // 2)

        def last_hop(b_off, way, step, now):
            if step == SIZES[third] // 2 and (turns.index(b_off) % 2 == 0) != (way == 1):
                return
            sem = new_sem()
            piece = chunk(part, index(second, b_off), index(third, -way * (step - 1)))
            started.append(send(piece, piece, device(moved(at, third, way), core), sem))

            def take(when):
                arrived(chunk(part, index(second, b_off), index(third, -way * step)), sem)
                if step < SIZES[third] // 2:
                    last_hop(b_off, way, step + 1, when)
                left[part, step] -= 1
                if left[part, step] == 0:
                    filled(part, step, when)

            at_time(link(now, third, way, chunk_bytes), take)

        def have(b_off, now):
            for way in (1, -1):
                last_hop(b_off, way, 1, now)

        def middle_hop(way, step, now):
            last = step == SIZES[second] // 2
            half = None if not last else (0 if way == 1 else 1)
            sem = new_sem()
            piece = chunk(part, index(second, -way * (step - 1)), at[third], half)
            started.append(send(piece, piece, device(moved(at, second, way), core), sem))

            def take(when):
                arrived(chunk(part, index(second, -way * step), at[third], half), sem)
                if not last:
                    middle_hop(way, step + 1, when)
                    have(-way * step, when)
                else:
                    left[part, "middle"] -= 1
                    if left[part, "middle"] == 0:
                        have(step, when)

            at_time(link(now, second, way, chunk_bytes // 2 if last else chunk_bytes), take)

        left[part, "middle"] = 2
        for step in range(1, SIZES[third] // 2 + 1):
            left[part, step] = SIZES[second] * (1 if step == SIZES[third] // 2 else 2)

        mine = []
        for d in range(1, SIZES[first]):
            sem = new_sem()
            slot = rows_of(part, *at)
            started.append(send(columns(part), slot, device(moved(at, first, d), core), sem))
            mine.append((rows_of(part, *moved(at, first, -d)), sem))

        def take(when):
            own[part].wait()
            for slot, sem in mine:
                arrived(slot, sem)
            for way in (1, -1):
                middle_hop(way, 1, when)
            have(0, when)

        at_time(START + HOP * SIZES[first] // 2 + 0.001 * part, take)

    def dot(a, b):
        return lax.dot_general(a, b, (((1,), (1,)), ((), ())), preferred_element_type=jnp.float32)

    def product(part, z):
        rhs = (out_z[:, :, z] if part == 2 else out[part, z]).reshape(width, PART)
        rhs_high = rhs.astype(jnp.bfloat16)
        rhs_low = (rhs - rhs_high.astype(jnp.float32)).astype(jnp.bfloat16)
        v_high = high[:, part * PART : (part + 1) * PART]
        v_low = low[:, part * PART : (part + 1) * PART]
        return dot(v_high, rhs_high) + (dot(v_high, rhs_low) + dot(v_low, rhs_high))

    def prepare_vectors():
        for copy in loads:
            copy.wait()
        for slot, sem in swaps:
            arrived(slot, sem)
        start = 0
        for ref in (stored, stored_in, cent, cent_in):
            count = ref.shape[0]
            top = ref[...].astype(jnp.bfloat16)
            high[start : start + count, :] = top
            low[start : start + count, :] = (ref[...] - top.astype(jnp.float32)).astype(jnp.bfloat16)
            start += count
        across = lax.broadcasted_iota(jnp.int32, (places, places), 1)
        down = lax.broadcasted_iota(jnp.int32, (places, places), 0)
        for n, ref in enumerate((ids, ids_in)):
            for i in range(lists):
                row = jnp.where(ref[i : i + 1, :] >= 0, jnp.float32(0), jnp.float32(LOW))
                column = jnp.sum(jnp.where(across == down, row, jnp.float32(0)), axis=1, keepdims=True)
                first = n * rows + i * places
                base[first : first + places, :] = jnp.broadcast_to(column, (places, width))
        base[2 * rows :, :] = jnp.zeros((2 * cents, width), jnp.float32)

        def fill(z, _):
            acc[z] = base[...]
            return 0

        lax.fori_loop(0, NZ, fill, 0)

    def prepare_picks():
        for copy in tables:
            copy.wait()
        at_slot = lax.broadcasted_iota(jnp.int32, home.shape, 1)
        row = lax.broadcasted_iota(jnp.int32, (probes.shape[1], width), 0)
        y_of = (lax.broadcasted_iota(jnp.int32, (probes.shape[1], width), 1) // 8) % NY
        for i in range(lists):
            held = jnp.max(jnp.where(home[...] == group * lists + i, at_slot, -1), axis=1, keepdims=True)
            for s in range(STEPS):
                hit = jnp.where(probes[s] == held, jnp.float32(0), jnp.float32(LOW))
                hit = jnp.max(hit, axis=1, keepdims=True)
                for zh in range(2):
                    line = jnp.where(row == y_of * 2 + zh, hit, jnp.float32(LOW))
                    pick[zh, s * lists + i : s * lists + i + 1, :] = jnp.max(line, axis=0, keepdims=True)

    def add_products(part, begin, stride, count):
        def one(k, _):
            z = lax.rem(at[Z] + (begin + NZ + k * stride), NZ)
            acc[z] += product(part, z)
            return 0

        lax.fori_loop(0, count, one, 0)

    def filled(part, step, when):
        if part == 0:
            if step == 1:
                span = (-1, 1, 3)
            elif step < NZ // 2:
                span = (-step, 2 * step, 2)
            else:
                span = (NZ // 2, 1, 1)
            later.append(lambda: add_products(0, *span))
        elif all(left[part, n] == 0 for n in range(1, SIZES[ORDERS[part][2]] // 2 + 1)):
            for n in range(0, NZ, 2):
                later.append(lambda n=n: add_products(part, n, 1, 2))

    for part in (1, 2, 0):
        run_part(part)
    for copy in own + tables + loads:
        copy.start()
    for src, dst in ((stored_hbm, stored_in), (cent_hbm, cent_in), (ids_hbm, ids_in)):
        sem = new_sem()
        started.append(send(src, dst, partner, sem))
        swaps.append((dst, sem))
    prepare_picks()
    while events:
        when, _, action = heapq.heappop(events)
        action(when)
        if used[0] == copies and later:
            later.pop(0)()
    for action in later:
        action()

    first_z = new_sem(NZ)

    def z_copy(d):
        return pltpu.make_async_remote_copy(
            src_ref=partial.at[lax.rem(at[Z] + d, NZ)],
            dst_ref=from_z.at[d - 1],
            send_sem=sends.at[first_z + d],
            recv_sem=recvs.at[first_z + d],
            device_id=device(moved(at, Z, d), core),
            device_id_type=pl.DeviceIdType.MESH,
        )

    def distance(k):
        return NZ // 2 + ((k + 1) // 2) * (1 - 2 * (k % 2))

    def finish(k, _):
        @pl.when(k > 0)
        def _():
            z_copy(distance(k - 1)).start()

        z = lax.rem(at[Z] + distance(k), NZ)
        total = acc.at[z]
        tops = []
        for i in range(lists):
            a = jnp.max(total[i * places : (i + 1) * places, :], axis=0, keepdims=True)
            b = jnp.max(total[rows + i * places : rows + (i + 1) * places, :], axis=0, keepdims=True)
            tops.append(jnp.maximum(a, b))
        partial[z, 0:1, :] = jnp.max(total[2 * rows :, :], axis=0, keepdims=True)
        chosen = pick[z // ZL]
        for s in range(STEPS):
            top = tops[0] + chosen[s * lists : s * lists + 1, :]
            for i in range(1, lists):
                top = jnp.maximum(top, tops[i] + chosen[s * lists + i : s * lists + i + 1, :])
            partial[z, s + 1 : s + 2, :] = top
        return 0

    lax.fori_loop(0, NZ, finish, 0)

    def most(value, landing):
        for i in range(landing.shape[0]):
            value = jnp.maximum(value, landing[i])
        return value

    def swap(axis, source, landing):
        copies = []
        for d in range(1, SIZES[axis]):
            copies.append(send(source, landing.at[d - 1], device(moved(at, axis, d), core), new_sem()))
        for copy in copies:
            copy.wait()

    for d in range(1, NZ):
        z_copy(d).wait()
    mid_z[...] = most(partial[at[Z]], from_z)
    swap(X, mid_z, from_x)
    mid_x[...] = most(mid_z[...], from_x)
    swap(Y, mid_x, from_y)
    best[...] = most(mid_x[...], from_y)
    for copy in started:
        copy.wait_send()


def local(queries, centroids, stored, vector_ids, list_home, probes):
    (x, y, z), core = place()
    lists, places = vector_ids.shape
    rows = lists * places
    cents = centroids.shape[0]
    f32 = jnp.float32
    width = NY * NX * 8
    piece = (1 + STEPS, width)
    held = 2 * rows + 2 * cents
    copies = 21 + 3 + 16 + 80 + NZ + NX + NY - 2
    best = pl.pallas_call(
        kernel,
        out_shape=jax.ShapeDtypeStruct(piece, f32),
        in_specs=[pl.BlockSpec(memory_space=pltpu.HBM)] * 6,
        out_specs=VMEM_SPEC,
        scratch_shapes=[
            pltpu.VMEM((2, NZ, NX, NY, 8, PART), f32),
            pltpu.VMEM((NX, NY, NZ, 8, PART), f32),
            pltpu.VMEM((cents, D), f32),
            pltpu.VMEM((rows, D), f32),
            pltpu.VMEM((lists, places), jnp.int32),
            pltpu.VMEM((1, list_home.shape[0]), jnp.int32),
            pltpu.VMEM((STEPS, probes.shape[0], probes.shape[2]), jnp.int32),
            pltpu.VMEM((cents, D), f32),
            pltpu.VMEM((rows, D), f32),
            pltpu.VMEM((lists, places), jnp.int32),
            pltpu.VMEM((held, D), jnp.bfloat16),
            pltpu.VMEM((held, D), jnp.bfloat16),
            pltpu.VMEM((held, width), f32),
            pltpu.VMEM((2, STEPS * lists, width), f32),
            pltpu.VMEM((NZ, held, width), f32),
            pltpu.VMEM((NZ,) + piece, f32),
            pltpu.VMEM((NZ - 1,) + piece, f32),
            pltpu.VMEM((NX - 1,) + piece, f32),
            pltpu.VMEM((NY - 1,) + piece, f32),
            pltpu.VMEM(piece, f32),
            pltpu.VMEM(piece, f32),
            pltpu.SemaphoreType.DMA((copies,)),
            pltpu.SemaphoreType.DMA((copies,)),
            pltpu.SemaphoreType.DMA((8,)),
        ],
        compiler_params=pltpu.CompilerParams(collective_id=0, has_side_effects=True, vmem_limit_bytes=66_900_000),
        name="search",
    )(queries, centroids, stored.reshape(rows, D), vector_ids, list_home.reshape(1, -1), jnp.transpose(probes, (1, 0, 2)))
    mine = lax.dynamic_slice_in_dim(best, (x * NY + y) * 8, 8, 1)
    return mine[0], mine[1:]


def solution(mesh):
    placed = (
        P(AXES, None),
        P(AXES, None),
        P("group", "member", None),
        P("group", "member"),
        P(),
        P(),
    )
    return jax.shard_map(
        local,
        mesh=mesh,
        in_specs=placed,
        out_specs=(P(AXES), P(None, AXES)),
        check_vma=False,
    )
```

```python
import heapq

import jax
import jax.numpy as jnp
from jax import lax
from jax.experimental import pallas as pl
from jax.experimental.pallas import tpu as pltpu
from jax.sharding import PartitionSpec as P

D = 768
STEPS = 3
AXES = ("group", "member")
LOW = -1e30
NX, NY, NZ, ZL = 4, 8, 8, 4
PART = D // 3
SIZES = (NX, NY, NZ)
X, Y, Z = 0, 1, 2
ORDERS = ((Y, X, Z), (Y, Z, X), (Z, X, Y))
RATE, HOP, START = 46000.0, 0.8, 0.9
VMEM_SPEC = pl.BlockSpec(memory_space=pltpu.VMEM)


def place():
    g, m = lax.axis_index("group"), lax.axis_index("member")
    x, y, core = (m // 2) % NX, g // 2, m % 2
    z = (g % 2) * ZL + m // (2 * NX)
    return [x, y, z], core


def device(at, core):
    x, y, z = at
    return (y * 2 + z // ZL, (z % ZL) * (2 * NX) + x * 2 + core)


def moved(at, axis, steps):
    size = SIZES[axis]
    out = list(at)
    out[axis] = lax.rem(at[axis] + (steps + size), size)
    return out


def greet(at, core):
    barrier = pltpu.get_barrier_semaphore()
    peers = [device(moved(at, axis, d), core) for axis in (X, Y, Z) for d in range(1, SIZES[axis])]
    return barrier, peers


def meet(barrier, peers):
    for peer in peers:
        pl.semaphore_signal(barrier, inc=1, device_id=peer, device_id_type=pl.DeviceIdType.MESH)
    pl.semaphore_wait(barrier, len(peers))


def kernel(q, cent_hbm, stored_hbm, ids_hbm, home_hbm, probes_hbm, best, out, cent, stored, ids, home, probes, cent_in, stored_in, ids_in, high, low, base, pick, acc,
           partial, from_z, from_x, from_y, mid_z, mid_x, sends, recvs, local_sems):
    at, core = place()
    group = lax.axis_index("group")
    lists, places = ids.shape
    rows = lists * places
    cents = cent.shape[0]
    width = NY * NX * 8
    barrier, peers = greet(at, core)
    partner = device(at, 1 - core)
    meet(barrier, peers + [partner])
    used = [0]
    started = []

    def send(src, dst, to, sem):
        copy = pltpu.make_async_remote_copy(
            src_ref=src,
            dst_ref=dst,
            send_sem=sends.at[sem],
            recv_sem=recvs.at[sem],
            device_id=to,
            device_id_type=pl.DeviceIdType.MESH,
        )
        copy.start()
        return copy

    def arrived(slot, sem):
        pltpu.make_async_remote_copy(
            src_ref=slot,
            dst_ref=slot,
            send_sem=sends.at[sem],
            recv_sem=recvs.at[sem],
            device_id=partner,
            device_id_type=pl.DeviceIdType.MESH,
        ).wait_recv()

    def new_sem(count=1):
        used[0] += count
        return used[0] - count

    def columns(part):
        return q.at[:, pl.ds(part * PART, PART)]

    own = []
    for part in range(3):
        own.append(pltpu.make_async_copy(columns(part), out.at[part, at[Z], at[Y], at[X]], local_sems.at[part]))
    loads = [
        pltpu.make_async_copy(stored_hbm, stored, local_sems.at[3]),
        pltpu.make_async_copy(cent_hbm, cent, local_sems.at[4]),
        pltpu.make_async_copy(ids_hbm, ids, local_sems.at[5]),
    ]

    tables = [
        pltpu.make_async_copy(home_hbm, home, local_sems.at[6]),
        pltpu.make_async_copy(probes_hbm, probes, local_sems.at[7]),
    ]

    events = []
    free = {}
    count = [0]

    def at_time(when, action):
        count[0] += 1
        heapq.heappush(events, (when, count[0], action))

    def link(now, axis, way, size):
        done = max(now, free.get((axis, way), 0.0)) + size / RATE
        free[axis, way] = done
        return done + HOP + START

    def index(axis, offset):
        return lax.rem(at[axis] + (offset + SIZES[axis]), SIZES[axis])

    def chunk(part, b, c, half=None):
        span = slice(None) if half is None else pl.ds(4 * half, 4)
        if part == 0:
            return out.at[0, c, span, b]
        if part == 1:
            return out.at[1, b, span, c]
        return out.at[2, span, c, b]

    chunk_bytes = 8 * 8 * PART * 4
    left = {}
    swaps = []

    def run_part(part):
        first, second, third = ORDERS[part]
        turns = [0]
        for d in range(1, SIZES[second] // 2):
            turns += [-d, d]
        turns.append(SIZES[second] // 2)

        def last_hop(b_off, way, step, now):
            if step == SIZES[third] // 2 and (turns.index(b_off) % 2 == 0) != (way == 1):
                return
            sem = new_sem()
            piece = chunk(part, index(second, b_off), index(third, -way * (step - 1)))
            started.append(send(piece, piece, device(moved(at, third, way), core), sem))

            def take(when):
                arrived(chunk(part, index(second, b_off), index(third, -way * step)), sem)
                if step < SIZES[third] // 2:
                    last_hop(b_off, way, step + 1, when)
                left[part, step] -= 1
                if left[part, step] == 0:
                    filled(part, step, when)

            at_time(link(now, third, way, chunk_bytes), take)

        def have(b_off, now):
            for way in (1, -1):
                last_hop(b_off, way, 1, now)

        def middle_hop(way, step, now):
            last = step == SIZES[second] // 2
            half = None if not last else (0 if way == 1 else 1)
            sem = new_sem()
            piece = chunk(part, index(second, -way * (step - 1)), at[third], half)
            started.append(send(piece, piece, device(moved(at, second, way), core), sem))

            def take(when):
                arrived(chunk(part, index(second, -way * step), at[third], half), sem)
                if not last:
                    middle_hop(way, step + 1, when)
                    have(-way * step, when)
                else:
                    left[part, "middle"] -= 1
                    if left[part, "middle"] == 0:
                        have(step, when)

            at_time(link(now, second, way, chunk_bytes // 2 if last else chunk_bytes), take)

        left[part, "middle"] = 2
        for step in range(1, SIZES[third] // 2 + 1):
            left[part, step] = SIZES[second] * (1 if step == SIZES[third] // 2 else 2)

        mine = []
        for d in range(1, SIZES[first]):
            sem = new_sem()
            slot = out.at[part, at[Z], at[Y], at[X]]
            started.append(send(columns(part), slot, device(moved(at, first, d), core), sem))
            fx, fy, fz = moved(at, first, -d)
            mine.append((out.at[part, fz, fy, fx], sem))

        def take(when):
            own[part].wait()
            for slot, sem in mine:
                arrived(slot, sem)
            for way in (1, -1):
                middle_hop(way, 1, when)
            have(0, when)

        at_time(START + HOP * SIZES[first] // 2 + 0.001 * part, take)

    def dot(a, b):
        return lax.dot_general(a, b, (((1,), (1,)), ((), ())), preferred_element_type=jnp.float32)

    def product(part, z):
        rhs = out[part, z].reshape(width, PART)
        rhs_high = rhs.astype(jnp.bfloat16)
        rhs_low = (rhs - rhs_high.astype(jnp.float32)).astype(jnp.bfloat16)
        v_high = high[:, part * PART : (part + 1) * PART]
        v_low = low[:, part * PART : (part + 1) * PART]
        return dot(v_high, rhs_high) + (dot(v_high, rhs_low) + dot(v_low, rhs_high))

    def prepare_vectors(when):
        for copy in loads:
            copy.wait()
        for slot, sem in swaps:
            arrived(slot, sem)
        start = 0
        for ref in (stored, stored_in, cent, cent_in):
            count = ref.shape[0]
            top = ref[...].astype(jnp.bfloat16)
            high[start : start + count, :] = top
            low[start : start + count, :] = (ref[...] - top.astype(jnp.float32)).astype(jnp.bfloat16)
            start += count
        across = lax.broadcasted_iota(jnp.int32, (places, places), 1)
        down = lax.broadcasted_iota(jnp.int32, (places, places), 0)
        for n, ref in enumerate((ids, ids_in)):
            for i in range(lists):
                row = jnp.where(ref[i : i + 1, :] >= 0, jnp.float32(0), jnp.float32(LOW))
                column = jnp.sum(jnp.where(across == down, row, jnp.float32(0)), axis=1, keepdims=True)
                first = n * rows + i * places
                base[first : first + places, :] = jnp.broadcast_to(column, (places, width))
        base[2 * rows :, :] = jnp.zeros((2 * cents, width), jnp.float32)

    def prepare_picks():
        for copy in tables:
            copy.wait()
        at_slot = lax.broadcasted_iota(jnp.int32, home.shape, 1)
        row = lax.broadcasted_iota(jnp.int32, (probes.shape[1], width), 0)
        y_of = lax.broadcasted_iota(jnp.int32, (probes.shape[1], width), 1) // (NX * 8)
        for i in range(lists):
            held = jnp.max(jnp.where(home[...] == group * lists + i, at_slot, -1), axis=1, keepdims=True)
            for s in range(STEPS):
                hit = jnp.where(probes[s] == held, jnp.float32(0), jnp.float32(LOW))
                hit = jnp.max(hit, axis=1, keepdims=True)
                for zh in range(2):
                    line = jnp.where(row == y_of * 2 + zh, hit, jnp.float32(LOW))
                    pick[zh, s * lists + i : s * lists + i + 1, :] = jnp.max(line, axis=0, keepdims=True)

    groups = ((-1, 1, 3), (-2, 4, 2), (-3, 6, 2), (NZ // 2, 1, 1))

    def add_products(part, group_at):
        begin, stride, count = groups[group_at]

        def one(k, _):
            z = lax.rem(at[Z] + (begin + NZ + k * stride), NZ)
            acc[z] = (base[...] if part == 0 else acc[z]) + product(part, z)
            return 0

        lax.fori_loop(0, count, one, 0)

    ready = set()
    later = []
    copies = 21 + 3 + 16 + 80

    def filled(part, step, when):
        if part == 0:
            add_products(0, step - 1)
            ready.add(step - 1)
        elif all(left[part, n] == 0 for n in range(1, SIZES[ORDERS[part][2]] // 2 + 1)):
            later.extend((n, part) for n in range(len(groups)))

    for part in (1, 2, 0):
        run_part(part)
    for copy in own + tables + loads:
        copy.start()
    for src, dst in ((stored_hbm, stored_in), (cent_hbm, cent_in), (ids_hbm, ids_in)):
        sem = new_sem()
        started.append(send(src, dst, partner, sem))
        swaps.append((dst, sem))
    prepare_picks()
    at_time(9.0, prepare_vectors)
    while events:
        when, _, action = heapq.heappop(events)
        action(when)
        if used[0] == copies:
            able = [item for item in later if item[0] in ready]
            if able:
                later.remove(able[0])
                add_products(able[0][1], able[0][0])
    for n, part in later:
        add_products(part, n)

    first_z = new_sem(NZ)

    def z_copy(d):
        return pltpu.make_async_remote_copy(
            src_ref=partial.at[lax.rem(at[Z] + d, NZ)],
            dst_ref=from_z.at[d - 1],
            send_sem=sends.at[first_z + d],
            recv_sem=recvs.at[first_z + d],
            device_id=device(moved(at, Z, d), core),
            device_id_type=pl.DeviceIdType.MESH,
        )

    def distance(k):
        return NZ // 2 + ((k + 1) // 2) * (1 - 2 * (k % 2))

    def finish(k, _):
        @pl.when(k > 0)
        def _():
            z_copy(distance(k - 1)).start()

        z = lax.rem(at[Z] + distance(k), NZ)
        total = acc.at[z]
        tops = []
        for i in range(lists):
            a = jnp.max(total[i * places : (i + 1) * places, :], axis=0, keepdims=True)
            b = jnp.max(total[rows + i * places : rows + (i + 1) * places, :], axis=0, keepdims=True)
            tops.append(jnp.maximum(a, b))
        partial[z, 0:1, :] = jnp.max(total[2 * rows :, :], axis=0, keepdims=True)
        chosen = pick[z // ZL]
        for s in range(STEPS):
            top = tops[0] + chosen[s * lists : s * lists + 1, :]
            for i in range(1, lists):
                top = jnp.maximum(top, tops[i] + chosen[s * lists + i : s * lists + i + 1, :])
            partial[z, s + 1 : s + 2, :] = top
        return 0

    lax.fori_loop(0, NZ, finish, 0)

    def most(value, landing):
        for i in range(landing.shape[0]):
            value = jnp.maximum(value, landing[i])
        return value

    def swap(axis, source, landing):
        copies = []
        for d in range(1, SIZES[axis]):
            copies.append(send(source, landing.at[d - 1], device(moved(at, axis, d), core), new_sem()))
        for copy in copies:
            copy.wait()

    for d in range(1, NZ):
        z_copy(d).wait()
    mid_z[...] = most(partial[at[Z]], from_z)
    swap(X, mid_z, from_x)
    mid_x[...] = most(mid_z[...], from_x)
    swap(Y, mid_x, from_y)
    best[...] = most(mid_x[...], from_y)
    for copy in started:
        copy.wait_send()


def local(queries, centroids, stored, vector_ids, list_home, probes):
    (x, y, z), core = place()
    lists, places = vector_ids.shape
    rows = lists * places
    cents = centroids.shape[0]
    f32 = jnp.float32
    width = NY * NX * 8
    piece = (1 + STEPS, width)
    held = 2 * rows + 2 * cents
    copies = 21 + 3 + 16 + 80 + NZ + NX + NY - 2
    best = pl.pallas_call(
        kernel,
        out_shape=jax.ShapeDtypeStruct(piece, f32),
        in_specs=[pl.BlockSpec(memory_space=pltpu.HBM)] * 6,
        out_specs=VMEM_SPEC,
        scratch_shapes=[
            pltpu.VMEM((3, NZ, NY, NX, 8, PART), f32),
            pltpu.VMEM((cents, D), f32),
            pltpu.VMEM((rows, D), f32),
            pltpu.VMEM((lists, places), jnp.int32),
            pltpu.VMEM((1, list_home.shape[0]), jnp.int32),
            pltpu.VMEM((STEPS, probes.shape[0], probes.shape[2]), jnp.int32),
            pltpu.VMEM((cents, D), f32),
            pltpu.VMEM((rows, D), f32),
            pltpu.VMEM((lists, places), jnp.int32),
            pltpu.VMEM((held, D), jnp.bfloat16),
            pltpu.VMEM((held, D), jnp.bfloat16),
            pltpu.VMEM((held, width), f32),
            pltpu.VMEM((2, STEPS * lists, width), f32),
            pltpu.VMEM((NZ, held, width), f32),
            pltpu.VMEM((NZ,) + piece, f32),
            pltpu.VMEM((NZ - 1,) + piece, f32),
            pltpu.VMEM((NX - 1,) + piece, f32),
            pltpu.VMEM((NY - 1,) + piece, f32),
            pltpu.VMEM(piece, f32),
            pltpu.VMEM(piece, f32),
            pltpu.SemaphoreType.DMA((copies,)),
            pltpu.SemaphoreType.DMA((copies,)),
            pltpu.SemaphoreType.DMA((8,)),
        ],
        compiler_params=pltpu.CompilerParams(collective_id=0, has_side_effects=True, vmem_limit_bytes=66_900_000),
        name="search",
    )(queries, centroids, stored.reshape(rows, D), vector_ids, list_home.reshape(1, -1), jnp.transpose(probes, (1, 0, 2)))
    mine = lax.dynamic_slice_in_dim(best, (y * NX + x) * 8, 8, 1)
    return mine[0], mine[1:]


def solution(mesh):
    placed = (
        P(AXES, None),
        P(AXES, None),
        P("group", "member", None),
        P("group", "member"),
        P(),
        P(),
    )
    return jax.shard_map(
        local,
        mesh=mesh,
        in_specs=placed,
        out_specs=(P(AXES), P(None, AXES)),
        check_vma=False,
    )
```

```python
import heapq

import jax
import jax.numpy as jnp
from jax import lax
from jax.experimental import pallas as pl
from jax.experimental.pallas import tpu as pltpu
from jax.sharding import PartitionSpec as P

D = 768
STEPS = 3
AXES = ("group", "member")
LOW = -1e30
NX, NY, NZ, ZL = 4, 8, 8, 4
PART = D // 3
SIZES = (NX, NY, NZ)
X, Y, Z = 0, 1, 2
ORDERS = ((Y, X, Z), (Y, Z, X), (Z, X, Y))
RATE, HOP, START = 46000.0, 0.8, 0.9
VMEM_SPEC = pl.BlockSpec(memory_space=pltpu.VMEM)


def place():
    g, m = lax.axis_index("group"), lax.axis_index("member")
    x, y, core = (m // 2) % NX, g // 2, m % 2
    z = (g % 2) * ZL + m // (2 * NX)
    return [x, y, z], core


def device(at, core):
    x, y, z = at
    return (y * 2 + z // ZL, (z % ZL) * (2 * NX) + x * 2 + core)


def moved(at, axis, steps):
    size = SIZES[axis]
    out = list(at)
    out[axis] = lax.rem(at[axis] + (steps + size), size)
    return out


def greet(at, core):
    barrier = pltpu.get_barrier_semaphore()
    peers = [device(moved(at, axis, d), core) for axis in (X, Y, Z) for d in range(1, SIZES[axis])]
    return barrier, peers


def meet(barrier, peers):
    for peer in peers:
        pl.semaphore_signal(barrier, inc=1, device_id=peer, device_id_type=pl.DeviceIdType.MESH)
    pl.semaphore_wait(barrier, len(peers))


def kernel(q, cent_hbm, stored_hbm, ids_hbm, home_hbm, probes_hbm, best, out, cent, stored, ids, home, probes, cent_in, stored_in, ids_in, high, low, base, pick, acc,
           partial, from_z, from_x, from_y, mid_z, mid_x, sends, recvs, local_sems):
    at, core = place()
    group = lax.axis_index("group")
    lists, places = ids.shape
    rows = lists * places
    cents = cent.shape[0]
    width = NY * NX * 8
    barrier, peers = greet(at, core)
    partner = device(at, 1 - core)
    meet(barrier, peers + [partner])
    used = [0]
    started = []

    def send(src, dst, to, sem):
        copy = pltpu.make_async_remote_copy(
            src_ref=src,
            dst_ref=dst,
            send_sem=sends.at[sem],
            recv_sem=recvs.at[sem],
            device_id=to,
            device_id_type=pl.DeviceIdType.MESH,
        )
        copy.start()
        return copy

    def arrived(slot, sem):
        pltpu.make_async_remote_copy(
            src_ref=slot,
            dst_ref=slot,
            send_sem=sends.at[sem],
            recv_sem=recvs.at[sem],
            device_id=partner,
            device_id_type=pl.DeviceIdType.MESH,
        ).wait_recv()

    def new_sem(count=1):
        used[0] += count
        return used[0] - count

    def columns(part):
        return q.at[:, pl.ds(part * PART, PART)]

    own = []
    for part in range(3):
        own.append(pltpu.make_async_copy(columns(part), out.at[part, at[Z], at[Y], at[X]], local_sems.at[part]))
    loads = [
        pltpu.make_async_copy(stored_hbm, stored, local_sems.at[3]),
        pltpu.make_async_copy(cent_hbm, cent, local_sems.at[4]),
        pltpu.make_async_copy(ids_hbm, ids, local_sems.at[5]),
    ]

    tables = [
        pltpu.make_async_copy(home_hbm, home, local_sems.at[6]),
        pltpu.make_async_copy(probes_hbm, probes, local_sems.at[7]),
    ]

    events = []
    free = {}
    count = [0]

    def at_time(when, action):
        count[0] += 1
        heapq.heappush(events, (when, count[0], action))

    def link(now, axis, way, size):
        done = max(now, free.get((axis, way), 0.0)) + size / RATE
        free[axis, way] = done
        return done + HOP + START

    def index(axis, offset):
        return lax.rem(at[axis] + (offset + SIZES[axis]), SIZES[axis])

    def chunk(part, b, c, half=None):
        span = slice(None) if half is None else pl.ds(4 * half, 4)
        if part == 0:
            return out.at[0, c, span, b]
        if part == 1:
            return out.at[1, b, span, c]
        return out.at[2, span, c, b]

    chunk_bytes = 8 * 8 * PART * 4
    left = {}
    swaps = []

    def run_part(part):
        first, second, third = ORDERS[part]
        turns = [0]
        for d in range(1, SIZES[second] // 2):
            turns += [-d, d]
        turns.append(SIZES[second] // 2)

        def last_hop(b_off, way, step, now):
            if step == SIZES[third] // 2 and (turns.index(b_off) % 2 == 0) != (way == 1):
                return
            sem = new_sem()
            piece = chunk(part, index(second, b_off), index(third, -way * (step - 1)))
            started.append(send(piece, piece, device(moved(at, third, way), core), sem))

            def take(when):
                arrived(chunk(part, index(second, b_off), index(third, -way * step)), sem)
                if step < SIZES[third] // 2:
                    last_hop(b_off, way, step + 1, when)
                left[part, step] -= 1
                if part == 0 and left[part, step] == 0:
                    filled(step - 1)

            at_time(link(now, third, way, chunk_bytes), take)

        def have(b_off, now):
            for way in (1, -1):
                last_hop(b_off, way, 1, now)

        def middle_hop(way, step, now):
            last = step == SIZES[second] // 2
            half = None if not last else (0 if way == 1 else 1)
            sem = new_sem()
            piece = chunk(part, index(second, -way * (step - 1)), at[third], half)
            started.append(send(piece, piece, device(moved(at, second, way), core), sem))

            def take(when):
                arrived(chunk(part, index(second, -way * step), at[third], half), sem)
                if not last:
                    middle_hop(way, step + 1, when)
                    have(-way * step, when)
                else:
                    left[part, "middle"] -= 1
                    if left[part, "middle"] == 0:
                        have(step, when)

            at_time(link(now, second, way, chunk_bytes // 2 if last else chunk_bytes), take)

        left[part, "middle"] = 2
        for step in range(1, SIZES[third] // 2 + 1):
            left[part, step] = SIZES[second] * (1 if step == SIZES[third] // 2 else 2)

        mine = []
        for d in range(1, SIZES[first]):
            sem = new_sem()
            slot = out.at[part, at[Z], at[Y], at[X]]
            started.append(send(columns(part), slot, device(moved(at, first, d), core), sem))
            fx, fy, fz = moved(at, first, -d)
            mine.append((out.at[part, fz, fy, fx], sem))

        def take(when):
            own[part].wait()
            for slot, sem in mine:
                arrived(slot, sem)
            for way in (1, -1):
                middle_hop(way, 1, when)
            have(0, when)

        at_time(START + HOP * SIZES[first] // 2 + 0.001 * part, take)

    def dot(a, b):
        return lax.dot_general(a, b, (((1,), (1,)), ((), ())), preferred_element_type=jnp.float32)

    def product(part, z):
        rhs = out[part, z].reshape(width, PART)
        rhs_high = rhs.astype(jnp.bfloat16)
        rhs_low = (rhs - rhs_high.astype(jnp.float32)).astype(jnp.bfloat16)
        v_high = high[:, part * PART : (part + 1) * PART]
        v_low = low[:, part * PART : (part + 1) * PART]
        return dot(v_high, rhs_high) + (dot(v_high, rhs_low) + dot(v_low, rhs_high))

    def prepare_vectors(when):
        for copy in loads:
            copy.wait()
        for slot, sem in swaps:
            arrived(slot, sem)
        start = 0
        for ref in (stored, stored_in, cent, cent_in):
            count = ref.shape[0]
            top = ref[...].astype(jnp.bfloat16)
            high[start : start + count, :] = top
            low[start : start + count, :] = (ref[...] - top.astype(jnp.float32)).astype(jnp.bfloat16)
            start += count
        across = lax.broadcasted_iota(jnp.int32, (places, places), 1)
        down = lax.broadcasted_iota(jnp.int32, (places, places), 0)
        for n, ref in enumerate((ids, ids_in)):
            for i in range(lists):
                row = jnp.where(ref[i : i + 1, :] >= 0, jnp.float32(0), jnp.float32(LOW))
                column = jnp.sum(jnp.where(across == down, row, jnp.float32(0)), axis=1, keepdims=True)
                first = n * rows + i * places
                base[first : first + places, :] = jnp.broadcast_to(column, (places, width))
        base[2 * rows :, :] = jnp.zeros((2 * cents, width), jnp.float32)

    def prepare_picks():
        for copy in tables:
            copy.wait()
        at_slot = lax.broadcasted_iota(jnp.int32, home.shape, 1)
        row = lax.broadcasted_iota(jnp.int32, (probes.shape[1], width), 0)
        y_of = lax.broadcasted_iota(jnp.int32, (probes.shape[1], width), 1) // (NX * 8)
        for i in range(lists):
            held = jnp.max(jnp.where(home[...] == group * lists + i, at_slot, -1), axis=1, keepdims=True)
            for s in range(STEPS):
                hit = jnp.where(probes[s] == held, jnp.float32(0), jnp.float32(LOW))
                hit = jnp.max(hit, axis=1, keepdims=True)
                for zh in range(2):
                    line = jnp.where(row == y_of * 2 + zh, hit, jnp.float32(LOW))
                    pick[zh, s * lists + i : s * lists + i + 1, :] = jnp.max(line, axis=0, keepdims=True)

    def first_third(begin, stride, count):
        def one(k, _):
            z = lax.rem(at[Z] + (begin + NZ + k * stride), NZ)
            acc[z] = base[...] + product(0, z)
            return 0

        lax.fori_loop(0, count, one, 0)

    def filled(step):
        if step == 0:
            first_third(-1, 1, 3)
        elif step < NZ // 2 - 1:
            first_third(-(step + 1), 2 * (step + 1), 2)
        else:
            first_third(NZ // 2, 1, 1)

    for part in (1, 2, 0):
        run_part(part)
    for copy in own + tables + loads:
        copy.start()
    for src, dst in ((stored_hbm, stored_in), (cent_hbm, cent_in), (ids_hbm, ids_in)):
        sem = new_sem()
        started.append(send(src, dst, partner, sem))
        swaps.append((dst, sem))
    prepare_picks()
    at_time(9.0, prepare_vectors)
    while events:
        when, _, action = heapq.heappop(events)
        action(when)

    first_z = new_sem(NZ)

    def z_copy(d):
        return pltpu.make_async_remote_copy(
            src_ref=partial.at[lax.rem(at[Z] + d, NZ)],
            dst_ref=from_z.at[d - 1],
            send_sem=sends.at[first_z + d],
            recv_sem=recvs.at[first_z + d],
            device_id=device(moved(at, Z, d), core),
            device_id_type=pl.DeviceIdType.MESH,
        )

    def distance(k):
        return NZ // 2 + ((k + 1) // 2) * (1 - 2 * (k % 2))

    def finish(k, _):
        @pl.when(k > 0)
        def _():
            z_copy(distance(k - 1)).start()

        z = lax.rem(at[Z] + distance(k), NZ)
        total = acc[z] + (product(1, z) + product(2, z))
        tops = []
        for i in range(lists):
            a = jnp.max(total[i * places : (i + 1) * places], axis=0, keepdims=True)
            b = jnp.max(total[rows + i * places : rows + (i + 1) * places], axis=0, keepdims=True)
            tops.append(jnp.maximum(a, b))
        partial[z, 0:1, :] = jnp.max(total[2 * rows :], axis=0, keepdims=True)
        chosen = pick[z // ZL]
        for s in range(STEPS):
            top = tops[0] + chosen[s * lists : s * lists + 1, :]
            for i in range(1, lists):
                top = jnp.maximum(top, tops[i] + chosen[s * lists + i : s * lists + i + 1, :])
            partial[z, s + 1 : s + 2, :] = top
        return 0

    lax.fori_loop(0, NZ, finish, 0)

    def most(value, landing):
        for i in range(landing.shape[0]):
            value = jnp.maximum(value, landing[i])
        return value

    def swap(axis, source, landing):
        copies = []
        for d in range(1, SIZES[axis]):
            copies.append(send(source, landing.at[d - 1], device(moved(at, axis, d), core), new_sem()))
        for copy in copies:
            copy.wait()

    for d in range(1, NZ):
        z_copy(d).wait()
    mid_z[...] = most(partial[at[Z]], from_z)
    swap(X, mid_z, from_x)
    mid_x[...] = most(mid_z[...], from_x)
    swap(Y, mid_x, from_y)
    best[...] = most(mid_x[...], from_y)
    for copy in started:
        copy.wait_send()


def local(queries, centroids, stored, vector_ids, list_home, probes):
    (x, y, z), core = place()
    lists, places = vector_ids.shape
    rows = lists * places
    cents = centroids.shape[0]
    f32 = jnp.float32
    width = NY * NX * 8
    piece = (1 + STEPS, width)
    held = 2 * rows + 2 * cents
    copies = 21 + 3 + 16 + 80 + NZ + NX + NY - 2
    best = pl.pallas_call(
        kernel,
        out_shape=jax.ShapeDtypeStruct(piece, f32),
        in_specs=[pl.BlockSpec(memory_space=pltpu.HBM)] * 6,
        out_specs=VMEM_SPEC,
        scratch_shapes=[
            pltpu.VMEM((3, NZ, NY, NX, 8, PART), f32),
            pltpu.VMEM((cents, D), f32),
            pltpu.VMEM((rows, D), f32),
            pltpu.VMEM((lists, places), jnp.int32),
            pltpu.VMEM((1, list_home.shape[0]), jnp.int32),
            pltpu.VMEM((STEPS, probes.shape[0], probes.shape[2]), jnp.int32),
            pltpu.VMEM((cents, D), f32),
            pltpu.VMEM((rows, D), f32),
            pltpu.VMEM((lists, places), jnp.int32),
            pltpu.VMEM((held, D), jnp.bfloat16),
            pltpu.VMEM((held, D), jnp.bfloat16),
            pltpu.VMEM((held, width), f32),
            pltpu.VMEM((2, STEPS * lists, width), f32),
            pltpu.VMEM((NZ, held, width), f32),
            pltpu.VMEM((NZ,) + piece, f32),
            pltpu.VMEM((NZ - 1,) + piece, f32),
            pltpu.VMEM((NX - 1,) + piece, f32),
            pltpu.VMEM((NY - 1,) + piece, f32),
            pltpu.VMEM(piece, f32),
            pltpu.VMEM(piece, f32),
            pltpu.SemaphoreType.DMA((copies,)),
            pltpu.SemaphoreType.DMA((copies,)),
            pltpu.SemaphoreType.DMA((8,)),
        ],
        compiler_params=pltpu.CompilerParams(collective_id=0, has_side_effects=True, vmem_limit_bytes=66_900_000),
        name="search",
    )(queries, centroids, stored.reshape(rows, D), vector_ids, list_home.reshape(1, -1), jnp.transpose(probes, (1, 0, 2)))
    first = (y * NX + x) * 8
    return lax.dynamic_slice(best, (0, first), (1, 8)).reshape(8), lax.dynamic_slice(best, (1, first), (STEPS, 8))


def solution(mesh):
    placed = (
        P(AXES, None),
        P(AXES, None),
        P("group", "member", None),
        P("group", "member"),
        P(),
        P(),
    )
    return jax.shard_map(
        local,
        mesh=mesh,
        in_specs=placed,
        out_specs=(P(AXES), P(None, AXES)),
        check_vma=False,
    )
```
